512 devices in a mesh: slab: 32 (over z, y_lo, core), filt: 16 (over x, y_hi).
Axes of the slice: x: 4, y: 8 (y_hi: 4, y_lo: 2; y = y_hi * 2 + y_lo), z: 8, core: 2. Of those that a mesh axis runs over, the one named last changes fastest.
Arguments:
- features: bfloat16 [64, 512, 256], P('slab', 'filt'), may hold values from -6 to 6
- first_weight: bfloat16 [27, 512, 512], P(None, 'filt'), may hold values from -0.0546875 to 0.0546875
- second_weight: bfloat16 [27, 512, 512], P(None, 'filt'), may hold values from -0.0546875 to 0.0546875
- head_weight: bfloat16 [8, 512], P(None, 'filt'), may hold values from -0.25 to 0.25
- labels: int32 [64, 256], P('slab'), may hold values from 0 to 7
Outputs:
- first_grad: float32 [27, 512, 512], P(None, 'filt', 'slab')
- second_grad: float32 [27, 512, 512], P(None, 'filt', 'slab')
The draws below stay inside these ranges and needn't reach their ends.
All inputs are finite; a program needn't handle non-finite values.
Results may differ from the reference program's by a relative error of at most 0.0075.
Values may be sent and summed in bfloat16 or wider, within the bound.
A program may use at most 64 MiB of HBM per device.

```python
import jax
import jax.numpy as jnp
from jax import lax

CHANNELS = 512
CLASSES = 8
HEIGHT = 32
WIDTH = 8
DEPTH = 64
PLANE = 256


def place_ends(entries, key, smallest, top_value):
    dims = entries.shape
    spot = [jax.random.randint(jax.random.fold_in(key, axis), (), 0, dims[axis]) for axis in range(len(dims))]
    entries = entries.at[tuple(spot)].set(smallest)
    longest = dims.index(max(dims))
    spot[longest] = (spot[longest] + 1) % dims[longest]
    return entries.at[tuple(spot)].set(top_value)


def levels(key, dims, cuts, smallest, largest):
    level = 1.0
    for position, parts in cuts:
        heights = jax.random.uniform(jax.random.fold_in(jax.random.fold_in(key, 6), position), (parts,), jnp.float32, smallest / len(cuts), largest / len(cuts))
        level = level * jnp.repeat(jnp.exp(heights), dims[position] // parts).reshape((-1,) + (1,) * (len(dims) - 1 - position))
    return level


def gaussian(rng, shape, scale, bound, cuts=(), kind=jnp.bfloat16):
    array = jax.random.normal(rng, shape, jnp.float32) * scale
    if len(cuts) > 0:
        array = levels(rng, shape, cuts, -0.22, 0.18) * array
    return jnp.clip(array, min=-bound, max=bound).astype(kind)


def setup_inputs(seed: int = 0) -> dict:
    seeds = jax.random.split(jax.random.key(seed), 6)
    return {
        "features": gaussian(seeds[0], (DEPTH, CHANNELS, PLANE), 1.0, 6.0, ((0, 32), (1, 16))),
        "first_weight": gaussian(seeds[1], (27, CHANNELS, CHANNELS), (27 * CHANNELS) ** -0.5, 0.0546875, ((1, 16),)),
        "second_weight": gaussian(seeds[2], (27, CHANNELS, CHANNELS), (27 * CHANNELS) ** -0.5, 0.0546875, ((1, 16),)),
        "head_weight": gaussian(seeds[3], (CLASSES, CHANNELS), CHANNELS ** -0.5, 0.25, ((1, 16),)),
        "labels": place_ends(jax.random.randint(seeds[4], (DEPTH, PLANE), 0, CLASSES), jax.random.fold_in(seeds[4], 1), 0, CLASSES - 1).astype(jnp.int32),
    }


def offset_list():
    found = []
    for depth_off in (-1, 0, 1):
        for row_off in (-1, 0, 1):
            for col_off in (-1, 0, 1):
                found.append((depth_off, row_off, col_off))
    return found

def silu_slope(values):
    sig = jax.nn.sigmoid(values)
    return sig * (1.0 + values * (1.0 - sig))

def shifted(volume, depth_off, row_off, col_off):
    planes = volume.shape[0]
    count_c = volume.shape[1]
    grid = volume.reshape(planes, count_c, HEIGHT, WIDTH)
    padded = jnp.pad(grid, ((1, 1), (0, 0), (1, 1), (1, 1)))
    moved = padded[1 + depth_off:1 + depth_off + planes, :, 1 + row_off:1 + row_off + HEIGHT, 1 + col_off:1 + col_off + WIDTH]
    return moved.reshape(planes, count_c, HEIGHT * WIDTH)

def forward_conv(volume, weight):
    summed = jnp.zeros((volume.shape[0], weight.shape[1], volume.shape[2]), jnp.float32)
    for number, offsets in enumerate(offset_list()):
        moved = shifted(volume, offsets[0], offsets[1], offsets[2]).astype(jnp.float32)
        summed = summed + jnp.einsum('fc,dcp->dfp', weight[number].astype(jnp.float32), moved, precision=lax.Precision.HIGHEST)
    return summed

def backward_conv(grad_out, weight):
    summed = jnp.zeros((grad_out.shape[0], weight.shape[2], grad_out.shape[2]), jnp.float32)
    for number, offsets in enumerate(offset_list()):
        moved = shifted(grad_out, -offsets[0], -offsets[1], -offsets[2]).astype(jnp.float32)
        summed = summed + jnp.einsum('fc,dfp->dcp', weight[number].astype(jnp.float32), moved, precision=lax.Precision.HIGHEST)
    return summed

def weight_grad(grad_out, volume):
    outer = grad_out.astype(jnp.float32)
    pieces = []
    for offsets in offset_list():
        moved = shifted(volume, offsets[0], offsets[1], offsets[2]).astype(jnp.float32)
        pieces.append(jnp.einsum('dfp,dcp->fc', outer, moved, precision=lax.Precision.HIGHEST))
    return jnp.stack(pieces)

def reference(features, first_weight, second_weight, head_weight, labels):
    pre_first = forward_conv(features, first_weight)
    hidden = jax.nn.silu(pre_first).astype(jnp.bfloat16)
    pre_second = forward_conv(hidden, second_weight)
    activated = jax.nn.silu(pre_second).astype(jnp.bfloat16)
    head_f = head_weight.astype(jnp.float32)
    logits = jnp.einsum('kc,dcp->dkp', head_f, activated.astype(jnp.float32), precision=lax.Precision.HIGHEST)
    powers = jnp.exp(logits)
    likely = powers / lax.optimization_barrier(jnp.sum(powers, axis=1, keepdims=True))
    classes_iota = jnp.arange(head_weight.shape[0], dtype=jnp.int32)
    onehot = (labels[:, None, :] == classes_iota[None, :, None]).astype(jnp.float32)
    logit_grad = (likely - onehot).astype(jnp.bfloat16)
    second_in = jnp.einsum('kc,dkp->dcp', head_f, logit_grad.astype(jnp.float32), precision=lax.Precision.HIGHEST)
    second_out_grad = (second_in * silu_slope(pre_second)).astype(jnp.bfloat16)
    second_grad = weight_grad(second_out_grad, hidden)
    hidden_grad = backward_conv(second_out_grad, second_weight)
    first_out_grad = (hidden_grad * silu_slope(pre_first)).astype(jnp.bfloat16)
    first_grad = weight_grad(first_out_grad, features)
    return (first_grad, second_grad)
```

```python
import functools

import jax
import jax.numpy as jnp
from jax import lax
from jax.experimental import pallas as pl
from jax.experimental.pallas import tpu as pltpu
from jax.sharding import PartitionSpec as P

MESH = pl.DeviceIdType.MESH
WIDTH = 8
HEIGHT = 32
PLANE = 256
NX, NY, NZ = 4, 4, 8
BLOCK = 32
ROWS = 27 * BLOCK
NINE = 9 * BLOCK
PADDED = 896
BF = jnp.bfloat16
F32 = jnp.float32


def sigmoid(v):
    return 1.0 / (1.0 + jnp.exp(-v))


def voxel_masks():
    p = lax.broadcasted_iota(jnp.int32, (BLOCK, PLANE), 1)
    return p // WIDTH, p % WIDTH


def offsets():
    return [(b, e) for b in (-1, 0, 1) for e in (-1, 0, 1)]


def inside(h, w, b, e):
    return (h + b >= 0) & (h + b < HEIGHT) & (w + e >= 0) & (w + e < WIDTH)


def fold_taps(stack, h, w):
    total = stack[4 * BLOCK : 5 * BLOCK]
    for n, (b, e) in enumerate(offsets()):
        if n == 4:
            continue
        moved = pltpu.roll(stack[n * BLOCK : (n + 1) * BLOCK], (-(8 * b + e)) % PLANE, 1)
        total = total + jnp.where(inside(h, w, b, e), moved, 0.0)
    return total


def spread_taps(stack_ref, plane, g, h, w):
    for n, (b, e) in enumerate(offsets()):
        if n == 4:
            moved = g
        else:
            moved = pltpu.roll(g, (8 * b + e) % PLANE, 1)
            moved = jnp.where(inside(h, w, -b, -e), moved, 0.0)
        stack_ref[pl.ds((3 - plane) * NINE + n * BLOCK, BLOCK), :] = moved.astype(BF)


def remote(src, dst, ssem, rsem, dev):
    return pltpu.make_async_remote_copy(
        src_ref=src, dst_ref=dst, send_sem=ssem, recv_sem=rsem, device_id=dev, device_id_type=MESH
    )


def kernel(
    feat_hbm, w1_hbm, w2_hbm, head_ref, labels_ref, out1_ref, out2_ref,
    feat, hid, w1, w2, w2t, oh_send, oh_recv, slope, ly, lx, g, stack,
    part, rx, qs, ry, wown, s1, r1, s2, r2, s3, r3,
    local_sem, gy_s, gy_r, gx_s, gx_r, oh_ss, oh_rs, c_s, c_r,
    ex_s, ex_r, ey_s, ey_r, a1_s, a1_r, a2_s, a2_r, a3_s, a3_r,
):
    s = lax.axis_index("slab")
    j = lax.axis_index("filt")
    n_slab = NZ * 4
    x, yh = j // NY, j % NY
    z, yl, core = s // 4, (s // 2) % 2, s % 2

    def at_y(k):
        return (yh + k) % NY

    def at_x(k):
        return (x + k) % NX

    def at_z(k):
        return (z + k) % NZ

    mate = s + 1 - 2 * core
    twin = s + 2 - 4 * yl
    low = (s + n_slab - 1) % n_slab
    high = (s + 1) % n_slab
    outer = (s + n_slab - 1 + 2 * core) % n_slab

    own = pltpu.make_async_copy(feat_hbm, feat.at[:, j], local_sem.at[0])
    own.start()
    cw1 = pltpu.make_async_copy(w1_hbm, w1, local_sem.at[1])
    cw1.start()
    cw2 = pltpu.make_async_copy(w2_hbm, w2.at[pl.ds(0, ROWS)], local_sem.at[2])
    cw2.start()

    barrier = pltpu.get_barrier_semaphore()
    peers = [(s, x * NY + at_y(k)) for k in (1, 2, 3)]
    peers += [(s, at_x(k) * NY + yh) for k in (1, 2, 3)]
    peers += [(mate, j), (outer, j), (twin, j)]
    peers += [(at_z(k) * 4 + yl * 2 + core, j) for k in range(1, NZ)]
    for dev in peers:
        pl.semaphore_signal(barrier, inc=1, device_id=dev, device_id_type=MESH)
    pl.semaphore_wait(barrier, len(peers))

    h, w = voxel_masks()

    def gather_start(vol, q):
        mine = vol.at[:, j]
        sent = []
        for k in (2, 1, 3):
            sent.append(remote(mine, mine, gy_s.at[q, k], gy_r.at[q, k], (s, x * NY + at_y(k))))
        for m in (2, 1, 3):
            sent.append(
                remote(mine, mine, gx_s.at[q, 0, m], gx_r.at[q, 0, m], (s, at_x(m) * NY + yh))
            )
        for c in sent:
            c.start()
        for k in (1, 3, 2):
            slot = vol.at[:, x * NY + at_y(NY - k)]
            remote(slot, slot, gy_s.at[q, k], gy_r.at[q, k], (s, j)).wait_recv()
            for m in (2, 1, 3):
                c = remote(slot, slot, gx_s.at[q, k, m], gx_r.at[q, k, m], (s, at_x(m) * NY + yh))
                c.start()
                sent.append(c)
        return sent

    def gather_end(vol, q, sent):
        for k in (0, 1, 3, 2):
            for m in (1, 3, 2):
                slot = vol.at[:, at_x(NX - m) * NY + at_y(NY - k)]
                remote(slot, slot, gx_s.at[q, k, m], gx_r.at[q, k, m], (s, j)).wait_recv()
        for c in sent:
            c.wait_send()

    def mm(a, b):
        return jnp.dot(a, b, preferred_element_type=F32)

    def flat(vol, d):
        return vol[d].reshape(512, PLANE)

    def conv(wt, vol, q):
        v0, v1 = flat(vol, 0), flat(vol, 1)
        minus, zero, plus = pl.ds(0, NINE), pl.ds(NINE, NINE), pl.ds(2 * NINE, NINE)
        oh_send[q, 0] = fold_taps(mm(wt[plus, :], v0), h, w)
        to_low = remote(oh_send.at[q, 0], oh_recv.at[q, 1], oh_ss.at[q, 0], oh_rs.at[q, 1], (low, j))
        to_low.start()
        oh_send[q, 1] = fold_taps(mm(wt[minus, :], v1), h, w)
        to_high = remote(
            oh_send.at[q, 1], oh_recv.at[q, 0], oh_ss.at[q, 1], oh_rs.at[q, 0], (high, j)
        )
        to_high.start()
        first = fold_taps(mm(wt[zero, :], v0) + mm(wt[plus, :], v1), h, w)
        second = fold_taps(mm(wt[minus, :], v0) + mm(wt[zero, :], v1), h, w)
        to_low.wait()
        to_high.wait()
        first = first + jnp.where(s > 0, oh_recv[q, 0], 0.0)
        second = second + jnp.where(s < n_slab - 1, oh_recv[q, 1], 0.0)
        return first, second

    own.wait()
    sent = gather_start(feat, 0)
    cw2.wait()
    w2[pl.ds(ROWS, PADDED - ROWS), :] = jnp.zeros((PADDED - ROWS, 512), BF)
    for blk in range(PADDED // 128):
        w2t[:, pl.ds(blk * 128, 128)] = w2[pl.ds(blk * 128, 128), :].T
    stack[pl.ds(4 * NINE, PADDED - ROWS), :] = jnp.zeros((PADDED - ROWS, PLANE), BF)
    cw1.wait()
    gather_end(feat, 0, sent)
    pre = conv(w1, feat, 0)
    for d in range(2):
        hid[d, j] = (pre[d] * sigmoid(pre[d])).astype(BF).reshape(2, 16, PLANE)
    sent = gather_start(hid, 1)
    for d in range(2):
        sig = sigmoid(pre[d])
        slope[d] = sig * (1.0 + pre[d] * (1.0 - sig))
    gather_end(hid, 1, sent)

    pre = conv(w2, hid, 1)
    head = head_ref[...]
    slopes = []
    for d in range(2):
        sig = sigmoid(pre[d])
        activated = (pre[d] * sig).astype(BF)
        ly[0, pl.ds(8 * d, 8), :] = mm(head, activated)
        slopes.append(sig * (1.0 + pre[d] * (1.0 - sig)))
    cys = [
        remote(ly.at[0], ly.at[k], c_s.at[0, k], c_r.at[0, k], (s, x * NY + at_y(k)))
        for k in (2, 1, 3)
    ]
    for c in cys:
        c.start()
    for c in cys:
        c.wait()
    lx[0] = (ly[0] + ly[2]) + (ly[1] + ly[3])
    cxs = [
        remote(lx.at[0], lx.at[k], c_s.at[1, k], c_r.at[1, k], (s, at_x(k) * NY + yh))
        for k in (2, 1, 3)
    ]
    for c in cxs:
        c.start()
    for c in cxs:
        c.wait()
    logits = (lx[0] + lx[2]) + (lx[1] + lx[3])
    classes = lax.broadcasted_iota(jnp.int32, (8, PLANE), 0)
    headf = head.astype(F32)
    for d in range(2):
        powers = jnp.exp(logits[8 * d : 8 * d + 8])
        likely = powers / jnp.sum(powers, axis=0, keepdims=True)
        onehot = jnp.where(labels_ref[pl.ds(d, 1), :] == classes, 1.0, 0.0)
        lg = (likely - onehot).astype(BF).astype(F32)
        back = lax.dot_general(headf, lg, (((0,), (0,)), ((), ())), preferred_element_type=F32)
        g[0, 1 + d] = (back * slopes[d]).astype(BF)

    def halo_start(q):
        a = remote(g.at[q, 1], g.at[q, 3], oh_ss.at[2 + q, 0], oh_rs.at[2 + q, 1], (low, j))
        b = remote(g.at[q, 2], g.at[q, 0], oh_ss.at[2 + q, 1], oh_rs.at[2 + q, 0], (high, j))
        a.start()
        b.start()
        for plane in (1, 2):
            spread_taps(stack, plane, g[q, plane].astype(F32), h, w)
        return a, b

    def halo_end(q, copies):
        for c in copies:
            c.wait()
        spread_taps(stack, 0, jnp.where(s > 0, g[q, 0].astype(F32), 0.0), h, w)
        spread_taps(stack, 3, jnp.where(s < n_slab - 1, g[q, 3].astype(F32), 0.0), h, w)

    halo_end(0, halo_start(0))

    def term(d):
        return stack[pl.ds(NINE * (1 - d), PADDED), :]

    for d in range(2):
        part[d] = mm(w2t[...], term(d)).astype(BF).reshape(NX, NY, BLOCK, PLANE)
    exs = []
    for k in (2, 1, 3, 0):
        for m in (2, 1, 3):
            c = remote(
                part.at[:, at_x(m), at_y(k)], rx.at[m, k], ex_s.at[m, k], ex_r.at[m, k],
                (s, at_x(m) * NY + yh),
            )
            c.start()
            exs.append(c)

    def outer_product(vol, cc):
        total = None
        for d in range(2):
            rows = vol[d, :, cc].reshape(256, PLANE)
            prod = lax.dot_general(
                rows, term(d), (((1,), (1,)), ((), ())), preferred_element_type=F32
            )
            total = prod if total is None else total + prod
        return total.reshape(16, 16, PADDED)

    def grad_start(vol, q):
        s1[q] = outer_product(vol, 1 - core).astype(BF).reshape(NZ, 2, 16, PADDED)
        c = remote(s1.at[q], r1.at[q], a1_s.at[q], a1_r.at[q], (mate, j))
        c.start()
        wown[q] = outer_product(vol, core).reshape(NZ, 2, 16, PADDED)
        return c

    order = (4, 3, 5, 2, 6, 1, 7, 0)

    def grad_second(q, c):
        c.wait()
        sent = []
        for k in order:
            zz = at_z(k)
            s2[q, k] = (wown[q, zz, 1 - yl] + r1[q, zz, 1 - yl].astype(F32)).astype(BF)
            c = remote(s2.at[q, k], r2.at[q, k], a2_s.at[q, k], a2_r.at[q, k], (twin, j))
            c.start()
            sent.append(c)
        return sent

    def grad_third(q, waits):
        sent = []
        for k, c in zip(order, waits):
            zz = at_z(k)
            c.wait()
            both = wown[q, zz, yl] + r1[q, zz, yl].astype(F32) + r2[q, k].astype(F32)
            if k == 0:
                wown[q, zz, yl] = both
            else:
                s3[q, k] = both.astype(BF)
                c = remote(
                    s3.at[q, k], r3.at[q, k], a3_s.at[q, k], a3_r.at[q, k],
                    (zz * 4 + yl * 2 + core, j),
                )
                c.start()
                sent.append(c)
        return sent

    def grad_end(q, waits, out):
        total = wown[q, z, yl]
        for c in waits:
            c.wait()
        for k in range(1, NZ):
            total = total + r3[q, k].astype(F32)
        out[...] = total

    d1 = grad_start(hid, 0)

    for c in exs:
        c.wait_send()
    eys = []
    mine = None
    for k in (2, 1, 3, 0):
        for m in (2, 1, 3):
            remote(rx.at[m, k], rx.at[m, k], ex_s.at[m, k], ex_r.at[m, k], (s, j)).wait_recv()
        total = part[:, x, at_y(k)].astype(F32)
        for m in (1, 2, 3):
            total = total + rx[m, k].astype(F32)
        if k == 0:
            mine = total
        else:
            qs[k] = total.astype(BF)
            c = remote(qs.at[k], ry.at[k], ey_s.at[k], ey_r.at[k], (s, x * NY + at_y(k)))
            c.start()
            eys.append(c)
    d2 = grad_second(0, d1)
    for c in eys:
        c.wait()
    mine = mine + ry[1].astype(F32) + ry[2].astype(F32) + ry[3].astype(F32)
    for d in range(2):
        g[1, 1 + d] = (mine[d] * slope[d]).astype(BF)
    halos = halo_start(1)
    d3 = grad_third(0, d2)
    halo_end(1, halos)
    f1 = grad_start(feat, 1)
    grad_end(0, d3, out2_ref)
    grad_end(1, grad_third(1, grad_second(1, f1)), out1_ref)


def shards(features, first_weight, second_weight, head_weight, labels):
    vmem = pl.BlockSpec(memory_space=pltpu.VMEM)
    hbm = pl.BlockSpec(memory_space=pl.ANY)
    dma = pltpu.SemaphoreType.DMA
    out = jax.ShapeDtypeStruct((16, PADDED), F32)
    first, second = pl.pallas_call(
        kernel,
        out_shape=(out, out),
        in_specs=[hbm, hbm, hbm, vmem, vmem],
        out_specs=(vmem, vmem),
        scratch_shapes=[
            pltpu.VMEM((2, 16, 2, 16, PLANE), BF),
            pltpu.VMEM((2, 16, 2, 16, PLANE), BF),
            pltpu.VMEM((ROWS, 512), BF),
            pltpu.VMEM((PADDED, 512), BF),
            pltpu.VMEM((512, PADDED), BF),
            pltpu.VMEM((2, 2, BLOCK, PLANE), F32),
            pltpu.VMEM((2, 2, BLOCK, PLANE), F32),
            pltpu.VMEM((2, BLOCK, PLANE), F32),
            pltpu.VMEM((4, 16, PLANE), F32),
            pltpu.VMEM((4, 16, PLANE), F32),
            pltpu.VMEM((2, 4, BLOCK, PLANE), BF),
            pltpu.VMEM((4 * NINE + PADDED - ROWS, PLANE), BF),
            pltpu.VMEM((2, NX, NY, BLOCK, PLANE), BF),
            pltpu.VMEM((NX, NY, 2, BLOCK, PLANE), BF),
            pltpu.VMEM((NY, 2, BLOCK, PLANE), BF),
            pltpu.VMEM((NY, 2, BLOCK, PLANE), BF),
            pltpu.VMEM((2, NZ, 2, 16, PADDED), F32),
            pltpu.VMEM((2, NZ, 2, 16, PADDED), BF),
            pltpu.VMEM((2, NZ, 2, 16, PADDED), BF),
            pltpu.VMEM((2, NZ, 16, PADDED), BF),
            pltpu.VMEM((2, NZ, 16, PADDED), BF),
            pltpu.VMEM((2, NZ, 16, PADDED), BF),
            pltpu.VMEM((2, NZ, 16, PADDED), BF),
            dma((3,)),
            dma((2, 4)), dma((2, 4)), dma((2, 4, 4)), dma((2, 4, 4)),
            dma((4, 2)), dma((4, 2)), dma((2, 4)), dma((2, 4)),
            dma((4, 4)), dma((4, 4)), dma((4,)), dma((4,)),
            dma((2,)), dma((2,)), dma((2, NZ)), dma((2, NZ)), dma((2, NZ)), dma((2, NZ)),
        ],
        compiler_params=pltpu.CompilerParams(
            collective_id=0, has_side_effects=True, vmem_limit_bytes=48 * 1024 * 1024
        ),
    )(
        features.reshape(2, 2, 16, PLANE),
        first_weight.reshape(ROWS, 512),
        second_weight.reshape(ROWS, 512),
        head_weight,
        labels,
    )
    return tuple(jnp.transpose(v[:, :ROWS]).reshape(27, BLOCK, 16) for v in (first, second))


def solution(mesh):
    placed = (
        P("slab", "filt", None),
        P(None, "filt", None),
        P(None, "filt", None),
        P(None, "filt"),
        P("slab", None),
    )
    return jax.shard_map(
        shards,
        mesh=mesh,
        in_specs=placed,
        out_specs=(P(None, "filt", "slab"), P(None, "filt", "slab")),
        check_vma=False,
    )
```

```python
import functools

import jax
import jax.numpy as jnp
from jax import lax
from jax.experimental import pallas as pl
from jax.experimental.pallas import tpu as pltpu
from jax.sharding import PartitionSpec as P

MESH = pl.DeviceIdType.MESH
WIDTH = 8
HEIGHT = 32
PLANE = 256
NX, NY, NZ = 4, 4, 8
BLOCK = 32
ROWS = 27 * BLOCK
NINE = 9 * BLOCK
PADDED = 896
BF = jnp.bfloat16
F32 = jnp.float32


def sigmoid(v):
    return 1.0 / (1.0 + jnp.exp(-v))


def voxel_masks():
    p = lax.broadcasted_iota(jnp.int32, (BLOCK, PLANE), 1)
    return p // WIDTH, p % WIDTH


def offsets():
    return [(b, e) for b in (-1, 0, 1) for e in (-1, 0, 1)]


def inside(h, w, b, e):
    return (h + b >= 0) & (h + b < HEIGHT) & (w + e >= 0) & (w + e < WIDTH)


def fold_taps(stack, h, w):
    total = stack[4 * BLOCK : 5 * BLOCK]
    for n, (b, e) in enumerate(offsets()):
        if n == 4:
            continue
        moved = pltpu.roll(stack[n * BLOCK : (n + 1) * BLOCK], (-(8 * b + e)) % PLANE, 1)
        total = total + jnp.where(inside(h, w, b, e), moved, 0.0)
    return total


def spread_taps(stack_ref, plane, g, h, w):
    base = pl.multiple_of((3 - plane) * NINE, BLOCK)
    for n, (b, e) in enumerate(offsets()):
        if n == 4:
            moved = g
        else:
            moved = pltpu.roll(g, (8 * b + e) % PLANE, 1)
            moved = jnp.where(inside(h, w, -b, -e), moved, 0.0)
        stack_ref[pl.ds(base + n * BLOCK, BLOCK), :] = moved.astype(BF)


def remote(src, dst, ssem, rsem, dev):
    return pltpu.make_async_remote_copy(
        src_ref=src, dst_ref=dst, send_sem=ssem, recv_sem=rsem, device_id=dev, device_id_type=MESH
    )


def kernel(
    feat_hbm, w1_hbm, w2_hbm, head_hbm, labels_hbm, out1_ref, out2_ref,
    feat, hid, near, w1, w2, w2t, head_v, labels_v, oh_send, oh_recv, slope, ly, lx, g,
    stack, stack2, part, rx, qs, ry, wown, s1, r1, s2, r2, s3, r3,
    local_sem, gy_s, gy_r, gx_s, gx_r, oh_ss, oh_rs, nr_s, nr_r, c_s, c_r,
    ex_s, ex_r, ey_s, ey_r, a1_s, a1_r, a2_s, a2_r, a3_s, a3_r,
):
    s = lax.axis_index("slab")
    j = lax.axis_index("filt")
    n_slab = NZ * 4
    x, yh = j // NY, j % NY
    z, yl, core = s // 4, (s // 2) % 2, s % 2

    def at_y(k):
        return (yh + k) % NY

    def at_x(k):
        return (x + k) % NX

    def at_z(k):
        return (z + k) % NZ

    mate = s + 1 - 2 * core
    twin = s + 2 - 4 * yl
    outer = (s + n_slab - 1 + 2 * core) % n_slab
    valid = (s > 0) & (s < n_slab - 1)

    locals_ = [
        pltpu.make_async_copy(feat_hbm.at[core], feat.at[0, j], local_sem.at[0]),
        pltpu.make_async_copy(feat_hbm.at[1 - core], feat.at[1, j], local_sem.at[1]),
        pltpu.make_async_copy(w2_hbm, w2.at[pl.ds(0, ROWS)], local_sem.at[2]),
        pltpu.make_async_copy(w1_hbm, w1, local_sem.at[3]),
        pltpu.make_async_copy(head_hbm, head_v, local_sem.at[4]),
        pltpu.make_async_copy(labels_hbm, labels_v, local_sem.at[5]),
    ]

    barrier = pltpu.get_barrier_semaphore()
    peers = [(s, x * NY + at_y(k)) for k in (2, 1, 3)]
    peers += [(s, at_x(k) * NY + yh) for k in (2, 1, 3)]
    peers += [(at_z(k) * 4 + yl * 2 + core, j) for k in (4, 3, 5, 2, 6, 1, 7)]
    peers += [(outer, j), (twin, j), (mate, j)]
    for dev in peers:
        pl.semaphore_signal(barrier, inc=1, device_id=dev, device_id_type=MESH)
    for c in locals_:
        c.start()
    pl.semaphore_wait(barrier, len(peers))

    h, w = voxel_masks()
    tail = []

    def gather_own(src, vol, q, p):
        dst = vol.at[p, j]
        sent = []
        for k in (2, 1, 3):
            sent.append(
                remote(src, dst, gy_s.at[q, p, k], gy_r.at[q, p, k], (s, x * NY + at_y(k)))
            )
        for m in (2, 1, 3):
            sent.append(
                remote(src, dst, gx_s.at[q, p, 0, m], gx_r.at[q, p, 0, m], (s, at_x(m) * NY + yh))
            )
        for c in sent:
            c.start()
        tail.extend(sent)

    def gather_forward(vol, q, p):
        for k in (1, 3, 2):
            slot = vol.at[p, x * NY + at_y(NY - k)]
            remote(slot, slot, gy_s.at[q, p, k], gy_r.at[q, p, k], (s, j)).wait_recv()
            for m in (2, 1, 3):
                c = remote(
                    slot, slot, gx_s.at[q, p, k, m], gx_r.at[q, p, k, m], (s, at_x(m) * NY + yh)
                )
                c.start()
                tail.append(c)

    def gather_end(vol, q, p):
        for k in (0, 1, 3, 2):
            for m in (1, 3, 2):
                slot = vol.at[p, at_x(NX - m) * NY + at_y(NY - k)]
                remote(slot, slot, gx_s.at[q, p, k, m], gx_r.at[q, p, k, m], (s, j)).wait_recv()

    def settle():
        for c in tail:
            c.wait_send()
        tail.clear()

    def mm(a, b):
        return jnp.dot(a, b, preferred_element_type=F32)

    def flat(vol, p):
        return vol[p].reshape(512, PLANE)

    away = pl.multiple_of((1 - core) * (2 * NINE), BLOCK)
    inward = pl.multiple_of(core * (2 * NINE), BLOCK)

    def conv(wt, vol, q):
        gather_end(vol, q, 0)
        vo = flat(vol, 0)
        oh_send[q, 0] = fold_taps(mm(wt[pl.ds(away, NINE), :], vo), h, w)
        to_outer = remote(
            oh_send.at[q, 0], oh_recv.at[q, 0], oh_ss.at[q, 0], oh_rs.at[q, 0], (outer, j)
        )
        to_outer.start()
        out_o = mm(wt[pl.ds(NINE, NINE), :], vo)
        out_i = mm(wt[pl.ds(inward, NINE), :], vo)
        gather_end(vol, q, 1)
        vi = flat(vol, 1)
        oh_send[q, 1] = fold_taps(mm(wt[pl.ds(inward, NINE), :], vi), h, w)
        to_mate = remote(
            oh_send.at[q, 1], oh_recv.at[q, 1], oh_ss.at[q, 1], oh_rs.at[q, 1], (mate, j)
        )
        to_mate.start()
        out_o = fold_taps(out_o + mm(wt[pl.ds(away, NINE), :], vi), h, w)
        out_i = fold_taps(out_i + mm(wt[pl.ds(NINE, NINE), :], vi), h, w)
        settle()
        to_outer.wait()
        yield out_o + jnp.where(valid, oh_recv[q, 0], 0.0)
        to_mate.wait()
        yield out_i + oh_recv[q, 1]

    def slope_of(v, sig):
        return sig * (1.0 + v * (1.0 - sig))

    for p in range(2):
        gather_own(feat_hbm.at[core + p - 2 * core * p], feat, 0, p)
    for p in range(2):
        gather_forward(feat, 0, p)
    for c in locals_:
        c.wait()
    w2[pl.ds(ROWS, PADDED - ROWS), :] = jnp.zeros((PADDED - ROWS, 512), BF)
    for blk in range(PADDED // 128):
        w2t[:, pl.ds(blk * 128, 128)] = w2[pl.ds(blk * 128, 128), :].T
    stack[pl.ds(4 * NINE, PADDED - ROWS), :] = jnp.zeros((PADDED - ROWS, PLANE), BF)
    stack2[pl.ds(0, NINE), :] = jnp.zeros((NINE, PLANE), BF)
    stack2[pl.ds(3 * NINE, NINE + PADDED - ROWS), :] = jnp.zeros((NINE + PADDED - ROWS, PLANE), BF)
    pre = []
    for p, v in enumerate(conv(w1, feat, 0)):
        hid[p, j] = (v * sigmoid(v)).astype(BF).reshape(2, 16, PLANE)
        gather_own(hid.at[p, j], hid, 1, p)
        pre.append(v)
    for p in range(2):
        slope[p] = slope_of(pre[p], sigmoid(pre[p]))
    for p in range(2):
        gather_forward(hid, 1, p)
    nears = [
        remote(feat.at[1], near.at[1], nr_s.at[1], nr_r.at[1], (mate, j)),
        remote(feat.at[0], near.at[0], nr_s.at[0], nr_r.at[0], (outer, j)),
    ]
    for c in nears:
        c.start()

    head = head_v[...]
    slopes = []
    for p, v in enumerate(conv(w2, hid, 1)):
        sig = sigmoid(v)
        ly[0, pl.ds(8 * p, 8), :] = mm(head, (v * sig).astype(BF))
        slopes.append(slope_of(v, sig))
    cys = [
        remote(ly.at[0], ly.at[k], c_s.at[0, k], c_r.at[0, k], (s, x * NY + at_y(k)))
        for k in (2, 1, 3)
    ]
    for c in cys:
        c.start()
    for c in cys:
        c.wait()
    lx[0] = (ly[0] + ly[2]) + (ly[1] + ly[3])
    cxs = [
        remote(lx.at[0], lx.at[k], c_s.at[1, k], c_r.at[1, k], (s, at_x(k) * NY + yh))
        for k in (2, 1, 3)
    ]
    for c in cxs:
        c.start()
    for c in cxs:
        c.wait()
    logits = (lx[0] + lx[2]) + (lx[1] + lx[3])
    classes = lax.broadcasted_iota(jnp.int32, (8, PLANE), 0)
    headf = head.astype(F32)
    labels = labels_v[...]
    halos = []
    gs = []
    for p in range(2):
        powers = jnp.exp(logits[8 * p : 8 * p + 8])
        likely = powers / jnp.sum(powers, axis=0, keepdims=True)
        row = jnp.where(core == p, labels[0:1], labels[1:2])
        onehot = jnp.where(row == classes, 1.0, 0.0)
        lg = (likely - onehot).astype(BF).astype(F32)
        back = lax.dot_general(headf, lg, (((0,), (0,)), ((), ())), preferred_element_type=F32)
        v = (back * slopes[p]).astype(BF)
        g[p] = v
        c = remote(
            g.at[p], g.at[2 + p], oh_ss.at[2, p], oh_rs.at[2, p], ((outer, mate)[p], j)
        )
        c.start()
        halos.append(c)
        gs.append(v.astype(F32))
    spread_taps(stack, 1 + core, gs[0], h, w)
    spread_taps(stack, 2 - core, gs[1], h, w)

    def term(ref, plane, rows=PADDED, skip=0):
        start = (2 - plane) * NINE + skip
        return ref[pl.ds(start if isinstance(start, int) else pl.multiple_of(start, BLOCK), rows), :]

    def project(p, plane):
        part[p] = mm(w2t[...], term(stack, plane)).astype(BF).reshape(NX, NY, BLOCK, PLANE)
        for k in (2, 1, 3, 0):
            for m in (2, 1, 3):
                c = remote(
                    part.at[p, at_x(m), at_y(k)], rx.at[p, m, k],
                    ex_s.at[p, m, k], ex_r.at[p, m, k], (s, at_x(m) * NY + yh),
                )
                c.start()
                tail.append(c)

    halos[1].wait()
    spread_taps(stack, 3 - 3 * core, g[3].astype(F32), h, w)
    project(1, 2 - core)
    halos[0].wait()
    spread_taps(stack, 3 * core, jnp.where(valid, g[2].astype(F32), 0.0), h, w)
    project(0, 1 + core)

    order = (4, 3, 5, 2, 6, 1, 7, 0)
    halves = (order[:4], order[4:])

    def outer_product(q, cc, ks):
        def rows(vol, p):
            picked = [vol[p, pl.ds(2 * at_z(k), 2), cc] for k in ks]
            return jnp.concatenate(picked, axis=0).reshape(32 * len(ks), PLANE)

        def prod(a, b):
            return lax.dot_general(a, b, (((1,), (1,)), ((), ())), preferred_element_type=F32)

        if q == 0:
            total = prod(rows(hid, 0), term(stack, 1 + core))
            total = total + prod(rows(hid, 1), term(stack, 2 - core))
        else:
            total = prod(rows(feat, 0), term(stack2, 1 + core))
            total = total + prod(rows(feat, 1), term(stack2, 2 - core))
            below = jnp.where(s > 0, rows(near, core), 0.0).astype(BF)
            above = jnp.where(s < n_slab - 1, rows(near, 1 - core), 0.0).astype(BF)
            low = total[:, :384] + prod(below, term(stack2, 0, 384))
            high = total[:, 512:] + prod(above, term(stack2, 3, 384, 512))
            total = jnp.concatenate([low, total[:, 384:512], high], axis=1)
        return total.reshape(len(ks), 2, 16, PADDED)

    def grad_first(q):
        sent = []
        for f, ks in enumerate(halves):
            here = pl.ds(4 * f, 4)
            s1[q, here] = outer_product(q, 1 - core, ks).astype(BF)
            c = remote(s1.at[q, here], r1.at[q, here], a1_s.at[q, f], a1_r.at[q, f], (mate, j))
            c.start()
            sent.append(c)
        return sent

    def grad_second(q, waits):
        sent = []
        for f, ks in enumerate(halves):
            wown[q, pl.ds(4 * f, 4)] = outer_product(q, core, ks)
            waits[f].wait()
            for n in range(4 * f, 4 * f + 4):
                s2[q, n] = (wown[q, n, 1 - yl] + r1[q, n, 1 - yl].astype(F32)).astype(BF)
                c = remote(s2.at[q, n], r2.at[q, n], a2_s.at[q, n], a2_r.at[q, n], (twin, j))
                c.start()
                sent.append(c)
        return sent

    def grad_third(q, waits):
        sent = []
        for n, k in enumerate(order):
            waits[n].wait()
            both = wown[q, n, yl] + r1[q, n, yl].astype(F32) + r2[q, n].astype(F32)
            if k == 0:
                wown[q, n, yl] = both
            else:
                s3[q, n] = both.astype(BF)
                c = remote(
                    s3.at[q, n], r3.at[q, n], a3_s.at[q, n], a3_r.at[q, n],
                    (at_z(k) * 4 + yl * 2 + core, j),
                )
                c.start()
                sent.append(c)
        return sent

    def grad_end(q, waits, out):
        total = wown[q, NZ - 1, yl]
        for n, c in enumerate(waits):
            c.wait()
            total = total + r3[q, n].astype(F32)
        out[...] = total

    mine = [None, None]
    eys = []

    def exchange_y(p):
        for k in (2, 1, 3, 0):
            total = part[p, x, at_y(k)].astype(F32)
            for m in (1, 3, 2):
                slot = rx.at[p, m, k]
                remote(slot, slot, ex_s.at[p, m, k], ex_r.at[p, m, k], (s, j)).wait_recv()
                total = total + rx[p, m, k].astype(F32)
            if k == 0:
                mine[p] = total
            else:
                qs[p, k] = total.astype(BF)
                c = remote(
                    qs.at[p, k], ry.at[p, k], ey_s.at[p, k], ey_r.at[p, k], (s, x * NY + at_y(k))
                )
                c.start()
                eys.append(c)

    d1 = grad_first(0)
    exchange_y(1)
    d2 = grad_second(0, d1)
    exchange_y(0)
    settle()
    for c in eys:
        c.wait()
    for p in (1, 0):
        v = mine[p]
        for k in (1, 2, 3):
            v = v + ry[p, k].astype(F32)
        v = (v * slope[p]).astype(BF).astype(F32)
        spread_taps(stack2, (1 + core, 2 - core)[p], v, h, w)
    for c in nears:
        c.wait()
    f1 = grad_first(1)
    d3 = grad_third(0, d2)
    f2 = grad_second(1, f1)
    grad_end(0, d3, out2_ref)
    grad_end(1, grad_third(1, f2), out1_ref)


def shards(features, first_weight, second_weight, head_weight, labels):
    vmem = pl.BlockSpec(memory_space=pltpu.VMEM)
    hbm = pl.BlockSpec(memory_space=pltpu.HBM)
    dma = pltpu.SemaphoreType.DMA
    out = jax.ShapeDtypeStruct((16, PADDED), F32)
    first, second = pl.pallas_call(
        kernel,
        out_shape=(out, out),
        in_specs=[hbm] * 5,
        out_specs=(vmem, vmem),
        scratch_shapes=[
            pltpu.VMEM((2, 16, 2, 16, PLANE), BF),
            pltpu.VMEM((2, 16, 2, 16, PLANE), BF),
            pltpu.VMEM((2, 16, 2, 16, PLANE), BF),
            pltpu.VMEM((ROWS, 512), BF),
            pltpu.VMEM((PADDED, 512), BF),
            pltpu.VMEM((512, PADDED), BF),
            pltpu.VMEM((8, BLOCK), BF),
            pltpu.VMEM((2, PLANE), jnp.int32),
            pltpu.VMEM((2, 2, BLOCK, PLANE), F32),
            pltpu.VMEM((2, 2, BLOCK, PLANE), F32),
            pltpu.VMEM((2, BLOCK, PLANE), F32),
            pltpu.VMEM((4, 16, PLANE), F32),
            pltpu.VMEM((4, 16, PLANE), F32),
            pltpu.VMEM((4, BLOCK, PLANE), BF),
            pltpu.VMEM((4 * NINE + PADDED - ROWS, PLANE), BF),
            pltpu.VMEM((4 * NINE + PADDED - ROWS, PLANE), BF),
            pltpu.VMEM((2, NX, NY, BLOCK, PLANE), BF),
            pltpu.VMEM((2, NX, NY, BLOCK, PLANE), BF),
            pltpu.VMEM((2, NY, BLOCK, PLANE), BF),
            pltpu.VMEM((2, NY, BLOCK, PLANE), BF),
            pltpu.VMEM((2, NZ, 2, 16, PADDED), F32),
            pltpu.VMEM((2, NZ, 2, 16, PADDED), BF),
            pltpu.VMEM((2, NZ, 2, 16, PADDED), BF),
            pltpu.VMEM((2, NZ, 16, PADDED), BF),
            pltpu.VMEM((2, NZ, 16, PADDED), BF),
            pltpu.VMEM((2, NZ, 16, PADDED), BF),
            pltpu.VMEM((2, NZ, 16, PADDED), BF),
            dma((6,)),
            dma((2, 2, 4)), dma((2, 2, 4)), dma((2, 2, 4, 4)), dma((2, 2, 4, 4)),
            dma((3, 2)), dma((3, 2)), dma((2,)), dma((2,)), dma((2, 4)), dma((2, 4)),
            dma((2, 4, 4)), dma((2, 4, 4)), dma((2, 4)), dma((2, 4)),
            dma((2, 2)), dma((2, 2)), dma((2, NZ)), dma((2, NZ)), dma((2, NZ)), dma((2, NZ)),
        ],
        compiler_params=pltpu.CompilerParams(
            collective_id=0, has_side_effects=True, vmem_limit_bytes=48 * 1024 * 1024
        ),
    )(
        features.reshape(2, 2, 16, PLANE),
        first_weight.reshape(ROWS, 512),
        second_weight.reshape(ROWS, 512),
        head_weight,
        labels,
    )
    return tuple(jnp.transpose(v[:, :ROWS]).reshape(27, BLOCK, 16) for v in (first, second))


def solution(mesh):
    placed = (
        P("slab", "filt", None),
        P(None, "filt", None),
        P(None, "filt", None),
        P(None, "filt"),
        P("slab", None),
    )
    return jax.shard_map(
        shards,
        mesh=mesh,
        in_specs=placed,
        out_specs=(P(None, "filt", "slab"), P(None, "filt", "slab")),
        check_vma=False,
    )
```

```python
import functools

import jax
import jax.numpy as jnp
from jax import lax
from jax.experimental import pallas as pl
from jax.experimental.pallas import tpu as pltpu
from jax.sharding import PartitionSpec as P

MESH = pl.DeviceIdType.MESH
WIDTH = 8
HEIGHT = 32
PLANE = 256
NX, NY, NZ = 4, 4, 8
BLOCK = 32
ROWS = 27 * BLOCK
NINE = 9 * BLOCK
PADDED = 896
BF = jnp.bfloat16
F32 = jnp.float32


def sigmoid(v):
    return 1.0 / (1.0 + jnp.exp(-v))


def voxel_masks():
    p = lax.broadcasted_iota(jnp.int32, (BLOCK, PLANE), 1)
    return p // WIDTH, p % WIDTH


def offsets():
    return [(b, e) for b in (-1, 0, 1) for e in (-1, 0, 1)]


def inside(h, w, b, e):
    return (h + b >= 0) & (h + b < HEIGHT) & (w + e >= 0) & (w + e < WIDTH)


def fold_taps(stack, h, w):
    total = stack[4 * BLOCK : 5 * BLOCK]
    for n, (b, e) in enumerate(offsets()):
        if n == 4:
            continue
        moved = pltpu.roll(stack[n * BLOCK : (n + 1) * BLOCK], (-(8 * b + e)) % PLANE, 1)
        total = total + jnp.where(inside(h, w, b, e), moved, 0.0)
    return total


def spread_taps(stack_ref, plane, g, h, w):
    base = pl.multiple_of((4 - plane) * NINE, BLOCK)
    for n, (b, e) in enumerate(offsets()):
        if n == 4:
            moved = g
        else:
            moved = pltpu.roll(g, (8 * b + e) % PLANE, 1)
            moved = jnp.where(inside(h, w, -b, -e), moved, 0.0)
        stack_ref[pl.ds(base + n * BLOCK, BLOCK), :] = moved.astype(BF)


def remote(src, dst, ssem, rsem, dev):
    return pltpu.make_async_remote_copy(
        src_ref=src, dst_ref=dst, send_sem=ssem, recv_sem=rsem, device_id=dev, device_id_type=MESH
    )


def kernel(
    feat_hbm, w1_hbm, w2_hbm, head_hbm, labels_hbm, out1_ref, out2_ref,
    feat, hid, feat_m, hid_m, near, w1, w2, w2t, head_v, labels_v, oh_send, oh_recv, slope, ly, ld, lx, g, g2,
    stack, stack2, part, rx, qs, ry, wown, s2, r2, r4, s3, r3,
    local_sem, gy_s, gy_r, gx_s, gx_r, oh_ss, oh_rs, nr_s, nr_r, m_s, m_r, g_s, g_r, c_s, c_r,
    ex_s, ex_r, ey_s, ey_r, a2_s, a2_r, a3_s, a3_r, a4_s, a4_r,
):
    s = lax.axis_index("slab")
    j = lax.axis_index("filt")
    n_slab = NZ * 4
    x, yh = j // NY, j % NY
    z, yl, core = s // 4, (s // 2) % 2, s % 2

    def at_y(k):
        return (yh + k) % NY

    def at_x(k):
        return (x + k) % NX

    def at_z(k):
        return (z + k) % NZ

    mate = s + 1 - 2 * core
    twin = s + 2 - 4 * yl
    outer = (s + n_slab - 1 + 2 * core) % n_slab
    outer_mate = outer + 1 - 2 * (1 - core)
    valid = (s > 0) & (s < n_slab - 1)
    far_valid = ((core == 1) | (s < n_slab - 2)) & ((core == 0) | (s > 1))

    def diagonal(k):
        return at_z(k) * 4 + (1 - yl) * 2 + core

    locals_ = [
        pltpu.make_async_copy(feat_hbm.at[core], feat.at[0, j], local_sem.at[0]),
        pltpu.make_async_copy(feat_hbm.at[1 - core], feat.at[1, j], local_sem.at[1]),
        pltpu.make_async_copy(w2_hbm, w2.at[pl.ds(0, ROWS)], local_sem.at[2]),
        pltpu.make_async_copy(w1_hbm, w1, local_sem.at[3]),
        pltpu.make_async_copy(head_hbm, head_v, local_sem.at[4]),
        pltpu.make_async_copy(labels_hbm, labels_v, local_sem.at[5]),
    ]

    barrier = pltpu.get_barrier_semaphore()
    peers = [(s, x * NY + at_y(k)) for k in (2, 1, 3)]
    peers += [(s, at_x(k) * NY + yh) for k in (2, 1, 3)]
    peers += [(at_z(k) * 4 + yl * 2 + core, j) for k in (4, 3, 5, 2, 6, 1, 7)]
    peers += [(s, at_x(m) * NY + at_y(2)) for m in (2, 1, 3)]
    peers += [(diagonal(1), j), (diagonal(7), j), (outer, j), (twin, j), (mate, j)]
    for dev in peers:
        pl.semaphore_signal(barrier, inc=1, device_id=dev, device_id_type=MESH)
    for c in locals_:
        c.start()
    pl.semaphore_wait(barrier, len(peers))

    h, w = voxel_masks()
    tail = []

    def gather_own(src, vol, q, p):
        dst = vol.at[p, j]
        sent = []
        for k in (2, 1, 3):
            sent.append(
                remote(src, dst, gy_s.at[q, p, k], gy_r.at[q, p, k], (s, x * NY + at_y(k)))
            )
        for m in (2, 1, 3):
            sent.append(
                remote(src, dst, gx_s.at[q, p, 0, m], gx_r.at[q, p, 0, m], (s, at_x(m) * NY + yh))
            )
        for c in sent:
            c.start()
        tail.extend(sent)

    def gather_forward(vol, q):
        for p, k in ((0, 1), (0, 3), (1, 1), (1, 3), (0, 2), (1, 2)):
            slot = vol.at[p, x * NY + at_y(NY - k)]
            remote(slot, slot, gy_s.at[q, p, k], gy_r.at[q, p, k], (s, j)).wait_recv()
            for m in (2, 1, 3):
                c = remote(
                    slot, slot, gx_s.at[q, p, k, m], gx_r.at[q, p, k, m], (s, at_x(m) * NY + yh)
                )
                c.start()
                tail.append(c)

    def gather_end(vol, q, p):
        for k in (0, 1, 3, 2):
            for m in (1, 3, 2):
                slot = vol.at[p, at_x(NX - m) * NY + at_y(NY - k)]
                remote(slot, slot, gx_s.at[q, p, k, m], gx_r.at[q, p, k, m], (s, j)).wait_recv()

    def settle():
        for c in tail:
            c.wait_send()
        tail.clear()

    def mm(a, b):
        return jnp.dot(a, b, preferred_element_type=F32)

    def flat(vol, p):
        return vol[p].reshape(512, PLANE)

    away = pl.multiple_of((1 - core) * (2 * NINE), BLOCK)
    inward = pl.multiple_of(core * (2 * NINE), BLOCK)

    nears = []
    halves = [[], []]

    def send_near(first, count):
        blocks = pl.ds(first, count)
        f = len(nears) // 2
        for n, (cls, dev) in enumerate(((1 - core, outer), (core, outer_mate))):
            c = remote(
                feat.at[0, blocks, cls], near.at[n, blocks], nr_s.at[f, n], nr_r.at[f, n], (dev, j)
            )
            c.start()
            nears.append(c)

    def send_half(vol, dst, q):
        for p in range(2):
            c = remote(vol.at[p, :, 1 - core], dst.at[p], m_s.at[q, p], m_r.at[q, p], (mate, j))
            c.start()
            halves[q].append(c)

    def conv(wt, vol, q):
        gather_end(vol, q, 0)
        vo = flat(vol, 0)
        oh_send[q, 0] = fold_taps(mm(wt[pl.ds(away, NINE), :], vo), h, w)
        to_outer = remote(
            oh_send.at[q, 0], oh_recv.at[q, 0], oh_ss.at[q, 0], oh_rs.at[q, 0], (outer, j)
        )
        to_outer.start()
        if q == 0:
            send_near(0, 6)
        out_o = mm(wt[pl.ds(NINE, NINE), :], vo)
        out_i = mm(wt[pl.ds(inward, NINE), :], vo)
        gather_end(vol, q, 1)
        vi = flat(vol, 1)
        oh_send[q, 1] = fold_taps(mm(wt[pl.ds(inward, NINE), :], vi), h, w)
        to_mate = remote(
            oh_send.at[q, 1], oh_recv.at[q, 1], oh_ss.at[q, 1], oh_rs.at[q, 1], (mate, j)
        )
        to_mate.start()
        send_half(vol, (feat_m, hid_m)[q], q)
        out_o = fold_taps(out_o + mm(wt[pl.ds(away, NINE), :], vi), h, w)
        out_i = fold_taps(out_i + mm(wt[pl.ds(NINE, NINE), :], vi), h, w)
        settle()
        to_outer.wait()
        yield out_o + jnp.where(valid, oh_recv[q, 0], 0.0)
        to_mate.wait()
        yield out_i + oh_recv[q, 1]

    def slope_of(v, sig):
        return sig * (1.0 + v * (1.0 - sig))

    for p in range(2):
        gather_own(feat_hbm.at[core + p - 2 * core * p], feat, 0, p)
    gather_forward(feat, 0)
    for c in locals_:
        c.wait()
    w2[pl.ds(ROWS, PADDED - ROWS), :] = jnp.zeros((PADDED - ROWS, 512), BF)
    for blk in range(PADDED // 128):
        w2t[:, pl.ds(blk * 128, 128)] = w2[pl.ds(blk * 128, 128), :].T
    stack[...] = jnp.zeros_like(stack)
    stack2[pl.ds(0, NINE), :] = jnp.zeros((NINE, PLANE), BF)
    stack2[pl.ds(5 * NINE, NINE + PADDED - ROWS), :] = jnp.zeros((NINE + PADDED - ROWS, PLANE), BF)
    pre = []
    for p, v in enumerate(conv(w1, feat, 0)):
        hid[p, j] = (v * sigmoid(v)).astype(BF).reshape(2, 16, PLANE)
        gather_own(hid.at[p, j], hid, 1, p)
        pre.append(v)
    for p in range(2):
        slope[p] = slope_of(pre[p], sigmoid(pre[p]))
    gather_forward(hid, 1)
    send_near(6, 10)

    head = head_v[...]
    slopes = []
    for p, v in enumerate(conv(w2, hid, 1)):
        sig = sigmoid(v)
        ly[0, pl.ds(8 * p, 8), :] = mm(head, (v * sig).astype(BF))
        slopes.append(slope_of(v, sig))
    cys = [
        remote(ly.at[0], ly.at[k], c_s.at[0, k], c_r.at[0, k], (s, x * NY + at_y(k)))
        for k in (1, 3)
    ]
    cds = [
        remote(ly.at[0], ld.at[m], c_s.at[2, m], c_r.at[2, m], (s, at_x(m) * NY + at_y(2)))
        for m in (2, 1, 3, 0)
    ]
    for c in cys + cds:
        c.start()
    for c in cys:
        c.wait()
    lx[0] = ly[0] + (ly[1] + ly[3])
    cxs = [
        remote(lx.at[0], lx.at[k], c_s.at[1, k], c_r.at[1, k], (s, at_x(k) * NY + yh))
        for k in (2, 1, 3)
    ]
    for c in cxs:
        c.start()
    for c in cds:
        c.wait()
    direct = (ld[0] + ld[2]) + (ld[1] + ld[3])
    for c in cxs:
        c.wait()
    logits = ((lx[0] + lx[2]) + (lx[1] + lx[3])) + direct
    classes = lax.broadcasted_iota(jnp.int32, (8, PLANE), 0)
    headf = head.astype(F32)
    labels = labels_v[...]
    halos = {}
    own_planes = (3 * core, 1 + core)
    mate_planes = (3 - 3 * core, 2 - core)
    gs = []
    for p in range(2):
        powers = jnp.exp(logits[8 * p : 8 * p + 8])
        likely = powers / jnp.sum(powers, axis=0, keepdims=True)
        row = jnp.where(core == p, labels[0:1], labels[1:2])
        onehot = jnp.where(row == classes, 1.0, 0.0)
        lg = (likely - onehot).astype(BF).astype(F32)
        back = lax.dot_general(headf, lg, (((0,), (0,)), ((), ())), preferred_element_type=F32)
        v = (back * slopes[p]).astype(BF)
        g[p] = v
        if p == 0:
            halos[4] = remote(g.at[0], g.at[4], g_s.at[4], g_r.at[4], (outer, j))
            halos[4].start()
        halos[2 + p] = remote(g.at[p], g.at[2 + p], g_s.at[2 + p], g_r.at[2 + p], (mate, j))
        halos[2 + p].start()
        gs.append(v.astype(F32))
    halos[5] = remote(g.at[0], g.at[5], g_s.at[5], g_r.at[5], (outer_mate, j))
    halos[5].start()
    for p in range(2):
        spread_taps(stack, own_planes[p], gs[p], h, w)

    def term(ref, plane, rows=PADDED, skip=0):
        start = (3 - plane) * NINE + skip
        return ref[pl.ds(start if isinstance(start, int) else pl.multiple_of(start, BLOCK), rows), :]

    def project(p, plane):
        part[p] = mm(w2t[...], term(stack, plane)).astype(BF).reshape(NX, NY, BLOCK, PLANE)
        for k in (2, 1, 3, 0):
            for m in (2, 1, 3):
                c = remote(
                    part.at[p, at_x(m), at_y(k)], rx.at[p, m, k],
                    ex_s.at[p, m, k], ex_r.at[p, m, k], (s, at_x(m) * NY + yh),
                )
                c.start()
                tail.append(c)

    halos[3].wait()
    spread_taps(stack, mate_planes[1], g[3].astype(F32), h, w)
    project(1, own_planes[1])
    halos[4].wait()
    spread_taps(stack, 5 * core - 1, jnp.where(valid, g[4].astype(F32), 0.0), h, w)
    project(0, own_planes[0])

    far = (4, 3, 5, 2, 6)

    def prod(a, b):
        return lax.dot_general(a, b, (((1,), (1,)), ((), ())), preferred_element_type=F32)

    def own_rows(vol, p):
        return vol[p, :, core].reshape(256, PLANE)

    def mate_rows(vol, p):
        return vol[p].reshape(256, PLANE)

    def grad_second(q):
        sent = {}

        def go(tag, k, src, dst, ss, rs, slab, yy):
            src[q, k] = wown[q, at_z(k), yy].astype(BF)
            c = remote(src.at[q, k], dst.at[q, k], ss.at[q, k], rs.at[q, k], (slab, j))
            c.start()
            sent[tag, k] = c

        for k in far:
            go(2, k, s2, r2, a2_s, a2_r, twin, 1 - yl)
        for k in (1, 7):
            go(4, k, s2, r4, a4_s, a4_r, diagonal(k), 1 - yl)
            go(3, k, s3, r3, a3_s, a3_r, at_z(k) * 4 + yl * 2 + core, yl)
        go(2, 0, s2, r2, a2_s, a2_r, twin, 1 - yl)
        return sent

    def grad_third(q, sent):
        for k in far:
            zz = at_z(k)
            sent[2, k].wait()
            s3[q, k] = (wown[q, zz, yl] + r2[q, k].astype(F32)).astype(BF)
            c = remote(
                s3.at[q, k], r3.at[q, k], a3_s.at[q, k], a3_r.at[q, k],
                (zz * 4 + yl * 2 + core, j),
            )
            c.start()
            sent[3, k] = c

    def grad_end(q, sent, out):
        total = wown[q, z, yl]
        for ref, tag, k in [(r2, 2, 0), (r4, 4, 1), (r4, 4, 7)] + [
            (r3, 3, k) for k in (1, 7, 4, 3, 5, 2, 6)
        ]:
            sent[tag, k].wait()
            total = total + ref[q, k].astype(F32)
        out[...] = total

    mine = [None, None]
    eys = []

    def exchange_y(p):
        for k in (2, 1, 3, 0):
            total = part[p, x, at_y(k)].astype(F32)
            for m in (1, 3, 2):
                slot = rx.at[p, m, k]
                remote(slot, slot, ex_s.at[p, m, k], ex_r.at[p, m, k], (s, j)).wait_recv()
                total = total + rx[p, m, k].astype(F32)
            if k == 0:
                mine[p] = total
            else:
                qs[p, k] = total.astype(BF)
                c = remote(
                    qs.at[p, k], ry.at[p, k], ey_s.at[p, k], ey_r.at[p, k], (s, x * NY + at_y(k))
                )
                c.start()
                eys.append(c)

    halos[2].wait()
    spread_taps(stack, mate_planes[0], g[2].astype(F32), h, w)
    halos[5].wait()
    spread_taps(stack, 4 - 5 * core, jnp.where(far_valid, g[5].astype(F32), 0.0), h, w)
    for c in halves[1]:
        c.wait()
    total = prod(own_rows(hid, 0), term(stack, own_planes[0]))
    total = total + prod(own_rows(hid, 1), term(stack, own_planes[1]))
    total = total + prod(mate_rows(hid_m, 0), term(stack, mate_planes[0]))
    total = total + prod(mate_rows(hid_m, 1), term(stack, mate_planes[1]))
    wown[0] = total.reshape(NZ, 2, 16, PADDED)
    exchange_y(1)
    exchange_y(0)
    second = grad_second(0)
    settle()
    swaps = []
    for p in (1, 0):
        for c in eys[3 * (1 - p) : 3 * (1 - p) + 3]:
            c.wait()
        v = mine[p]
        for k in (1, 2, 3):
            v = v + ry[p, k].astype(F32)
        v = (v * slope[p]).astype(BF)
        g2[p] = v
        c = remote(g2.at[p], g2.at[2 + p], g_s.at[p], g_r.at[p], (mate, j))
        c.start()
        swaps.append(c)
        spread_taps(stack2, own_planes[p], v.astype(F32), h, w)
    for c in nears + halves[0]:
        c.wait()
    total = prod(own_rows(feat, 0), term(stack2, own_planes[0]))
    swaps[0].wait()
    spread_taps(stack2, mate_planes[1], g2[3].astype(F32), h, w)
    total = total + prod(own_rows(feat, 1), term(stack2, own_planes[1]))
    swaps[1].wait()
    spread_taps(stack2, mate_planes[0], g2[2].astype(F32), h, w)
    total = total + prod(mate_rows(feat_m, 0), term(stack2, mate_planes[0]))
    total = total + prod(mate_rows(feat_m, 1), term(stack2, mate_planes[1]))
    below = jnp.where(s > 1, mate_rows(near, core), 0.0).astype(BF)
    above = jnp.where(s < n_slab - 2, mate_rows(near, 1 - core), 0.0).astype(BF)
    low = total[:, :384] + prod(below, term(stack2, -1, 384))
    high = total[:, 512:] + prod(above, term(stack2, 4, 384, 512))
    wown[1] = jnp.concatenate([low, total[:, 384:512], high], axis=1).reshape(NZ, 2, 16, PADDED)
    first = grad_second(1)
    grad_third(0, second)
    grad_third(1, first)
    grad_end(0, second, out2_ref)
    grad_end(1, first, out1_ref)


def shards(features, first_weight, second_weight, head_weight, labels):
    vmem = pl.BlockSpec(memory_space=pltpu.VMEM)
    hbm = pl.BlockSpec(memory_space=pltpu.HBM)
    dma = pltpu.SemaphoreType.DMA
    out = jax.ShapeDtypeStruct((16, PADDED), F32)
    first, second = pl.pallas_call(
        kernel,
        out_shape=(out, out),
        in_specs=[hbm] * 5,
        out_specs=(vmem, vmem),
        scratch_shapes=[
            pltpu.VMEM((2, 16, 2, 16, PLANE), BF),
            pltpu.VMEM((2, 16, 2, 16, PLANE), BF),
            pltpu.VMEM((2, 16, 16, PLANE), BF),
            pltpu.VMEM((2, 16, 16, PLANE), BF),
            pltpu.VMEM((2, 16, 16, PLANE), BF),
            pltpu.VMEM((ROWS, 512), BF),
            pltpu.VMEM((PADDED, 512), BF),
            pltpu.VMEM((512, PADDED), BF),
            pltpu.VMEM((8, BLOCK), BF),
            pltpu.VMEM((2, PLANE), jnp.int32),
            pltpu.VMEM((2, 2, BLOCK, PLANE), F32),
            pltpu.VMEM((2, 2, BLOCK, PLANE), F32),
            pltpu.VMEM((2, BLOCK, PLANE), F32),
            pltpu.VMEM((4, 16, PLANE), F32),
            pltpu.VMEM((4, 16, PLANE), F32),
            pltpu.VMEM((4, 16, PLANE), F32),
            pltpu.VMEM((6, BLOCK, PLANE), BF),
            pltpu.VMEM((4, BLOCK, PLANE), BF),
            pltpu.VMEM((6 * NINE + PADDED - ROWS, PLANE), BF),
            pltpu.VMEM((6 * NINE + PADDED - ROWS, PLANE), BF),
            pltpu.VMEM((2, NX, NY, BLOCK, PLANE), BF),
            pltpu.VMEM((2, NX, NY, BLOCK, PLANE), BF),
            pltpu.VMEM((2, NY, BLOCK, PLANE), BF),
            pltpu.VMEM((2, NY, BLOCK, PLANE), BF),
            pltpu.VMEM((2, NZ, 2, 16, PADDED), F32),
            pltpu.VMEM((2, NZ, 16, PADDED), BF),
            pltpu.VMEM((2, NZ, 16, PADDED), BF),
            pltpu.VMEM((2, NZ, 16, PADDED), BF),
            pltpu.VMEM((2, NZ, 16, PADDED), BF),
            pltpu.VMEM((2, NZ, 16, PADDED), BF),
            dma((6,)),
            dma((2, 2, 4)), dma((2, 2, 4)), dma((2, 2, 4, 4)), dma((2, 2, 4, 4)),
            dma((2, 2)), dma((2, 2)), dma((2, 2)), dma((2, 2)), dma((2, 2)), dma((2, 2)),
            dma((6,)), dma((6,)), dma((3, 4)), dma((3, 4)),
            dma((2, 4, 4)), dma((2, 4, 4)), dma((2, 4)), dma((2, 4)),
            dma((2, NZ)), dma((2, NZ)), dma((2, NZ)), dma((2, NZ)), dma((2, NZ)), dma((2, NZ)),
        ],
        compiler_params=pltpu.CompilerParams(
            collective_id=0, has_side_effects=True, vmem_limit_bytes=60 * 1024 * 1024
        ),
    )(
        features.reshape(2, 2, 16, PLANE),
        first_weight.reshape(ROWS, 512),
        second_weight.reshape(ROWS, 512),
        head_weight,
        labels,
    )
    return tuple(jnp.transpose(v[:, :ROWS]).reshape(27, BLOCK, 16) for v in (first, second))


def solution(mesh):
    placed = (
        P("slab", "filt", None),
        P(None, "filt", None),
        P(None, "filt", None),
        P(None, "filt"),
        P("slab", None),
    )
    return jax.shard_map(
        shards,
        mesh=mesh,
        in_specs=placed,
        out_specs=(P(None, "filt", "slab"), P(None, "filt", "slab")),
        check_vma=False,
    )
```

```python
import functools

import jax
import jax.numpy as jnp
from jax import lax
from jax.experimental import pallas as pl
from jax.experimental.pallas import tpu as pltpu
from jax.sharding import PartitionSpec as P

MESH = pl.DeviceIdType.MESH
WIDTH = 8
HEIGHT = 32
PLANE = 256
NX, NY, NZ = 4, 4, 8
BLOCK = 32
ROWS = 27 * BLOCK
NINE = 9 * BLOCK
PADDED = 896
BF = jnp.bfloat16
F32 = jnp.float32


def sigmoid(v):
    return 1.0 / (1.0 + jnp.exp(-v))


def voxel_masks():
    p = lax.broadcasted_iota(jnp.int32, (BLOCK, PLANE), 1)
    return p // WIDTH, p % WIDTH


def offsets():
    return [(b, e) for b in (-1, 0, 1) for e in (-1, 0, 1)]


def inside(h, w, b, e):
    return (h + b >= 0) & (h + b < HEIGHT) & (w + e >= 0) & (w + e < WIDTH)


def fold_taps(stack, h, w):
    total = stack[4 * BLOCK : 5 * BLOCK]
    for n, (b, e) in enumerate(offsets()):
        if n == 4:
            continue
        moved = pltpu.roll(stack[n * BLOCK : (n + 1) * BLOCK], (-(8 * b + e)) % PLANE, 1)
        total = total + jnp.where(inside(h, w, b, e), moved, 0.0)
    return total


def spread_taps(stack_ref, plane, g, h, w):
    base = pl.multiple_of((4 - plane) * NINE, BLOCK)
    for n, (b, e) in enumerate(offsets()):
        if n == 4:
            moved = g
        else:
            moved = pltpu.roll(g, (8 * b + e) % PLANE, 1)
            moved = jnp.where(inside(h, w, -b, -e), moved, 0.0)
        stack_ref[pl.ds(base + n * BLOCK, BLOCK), :] = moved.astype(BF)


def remote(src, dst, ssem, rsem, dev):
    return pltpu.make_async_remote_copy(
        src_ref=src, dst_ref=dst, send_sem=ssem, recv_sem=rsem, device_id=dev, device_id_type=MESH
    )


def kernel(
    feat_hbm, w1_hbm, w2_hbm, head_hbm, labels_hbm, out1_ref, out2_ref,
    feat, hid, feat_m, hid_m, near, w1, w2, w2t, head_v, labels_v, oh_send, oh_recv, slope, ly, lx, g, g2,
    stack, stack2, part, rx, qs, ry, wown, sz, rz, st, rt, s2, r2, r4, s3, r3,
    local_sem, gy_s, gy_r, gx_s, gx_r, oh_ss, oh_rs, nr_s, nr_r, m_s, m_r, g_s, g_r, c_s, c_r,
    ex_s, ex_r, ey_s, ey_r, dz_s, dz_r, a2_s, a2_r, a3_s, a3_r, a4_s, a4_r,
):
    s = lax.axis_index("slab")
    j = lax.axis_index("filt")
    n_slab = NZ * 4
    x, yh = j // NY, j % NY
    z, yl, core = s // 4, (s // 2) % 2, s % 2

    def at_y(k):
        return (yh + k) % NY

    def at_x(k):
        return (x + k) % NX

    def at_z(k):
        return (z + k) % NZ

    mate = s + 1 - 2 * core
    twin = s + 2 - 4 * yl
    outer = (s + n_slab - 1 + 2 * core) % n_slab
    outer_mate = outer + 1 - 2 * (1 - core)
    valid = (s > 0) & (s < n_slab - 1)
    far_valid = ((core == 1) | (s < n_slab - 2)) & ((core == 0) | (s > 1))

    def diagonal(k):
        return at_z(k) * 4 + (1 - yl) * 2 + core

    locals_ = [
        pltpu.make_async_copy(feat_hbm.at[core], feat.at[0, j], local_sem.at[0]),
        pltpu.make_async_copy(feat_hbm.at[1 - core], feat.at[1, j], local_sem.at[1]),
        pltpu.make_async_copy(w2_hbm, w2.at[pl.ds(0, ROWS)], local_sem.at[2]),
        pltpu.make_async_copy(w1_hbm, w1, local_sem.at[3]),
        pltpu.make_async_copy(head_hbm, head_v, local_sem.at[4]),
        pltpu.make_async_copy(labels_hbm, labels_v, local_sem.at[5]),
    ]

    barrier = pltpu.get_barrier_semaphore()
    peers = [(s, x * NY + at_y(k)) for k in (2, 1, 3)]
    peers += [(s, at_x(k) * NY + yh) for k in (2, 1, 3)]
    peers += [(at_z(k) * 4 + yl * 2 + core, j) for k in (4, 3, 5, 2, 6, 1, 7)]
    peers += [(diagonal(1), j), (diagonal(7), j), (outer, j), (twin, j), (mate, j)]
    for dev in peers:
        pl.semaphore_signal(barrier, inc=1, device_id=dev, device_id_type=MESH)
    for c in locals_:
        c.start()
    pl.semaphore_wait(barrier, len(peers))

    h, w = voxel_masks()
    tail = []

    def gather_own(src, vol, q, p):
        dst = vol.at[p, j]
        sent = []
        for k in (2, 1, 3):
            sent.append(
                remote(src, dst, gy_s.at[q, p, k], gy_r.at[q, p, k], (s, x * NY + at_y(k)))
            )
        for m in (2, 1, 3):
            sent.append(
                remote(src, dst, gx_s.at[q, p, 0, m], gx_r.at[q, p, 0, m], (s, at_x(m) * NY + yh))
            )
        for c in sent:
            c.start()
        tail.extend(sent)

    def gather_forward(vol, q):
        for p, k in ((0, 1), (0, 3), (1, 1), (1, 3), (0, 2), (1, 2)):
            slot = vol.at[p, x * NY + at_y(NY - k)]
            remote(slot, slot, gy_s.at[q, p, k], gy_r.at[q, p, k], (s, j)).wait_recv()
            for m in (2, 1, 3):
                c = remote(
                    slot, slot, gx_s.at[q, p, k, m], gx_r.at[q, p, k, m], (s, at_x(m) * NY + yh)
                )
                c.start()
                tail.append(c)

    def gather_end(vol, q, p):
        for k in (0, 1, 3, 2):
            for m in (1, 3, 2):
                slot = vol.at[p, at_x(NX - m) * NY + at_y(NY - k)]
                remote(slot, slot, gx_s.at[q, p, k, m], gx_r.at[q, p, k, m], (s, j)).wait_recv()

    def settle():
        for c in tail:
            c.wait_send()
        tail.clear()

    def mm(a, b):
        return jnp.dot(a, b, preferred_element_type=F32)

    def flat(vol, p):
        return vol[p].reshape(512, PLANE)

    away = pl.multiple_of((1 - core) * (2 * NINE), BLOCK)
    inward = pl.multiple_of(core * (2 * NINE), BLOCK)

    halves = [[], []]

    def send_near():
        sent = []
        for n, (cls, dev) in enumerate(((1 - core, outer), (core, outer_mate))):
            c = remote(feat.at[0, :, cls], near.at[n], nr_s.at[n], nr_r.at[n], (dev, j))
            c.start()
            sent.append(c)
        return sent

    def send_half(vol, dst, q):
        for p in range(2):
            c = remote(vol.at[p, :, 1 - core], dst.at[p], m_s.at[q, p], m_r.at[q, p], (mate, j))
            c.start()
            halves[q].append(c)

    def conv(wt, vol, q):
        gather_end(vol, q, 0)
        vo = flat(vol, 0)
        oh_send[q, 0] = fold_taps(mm(wt[pl.ds(away, NINE), :], vo), h, w)
        to_outer = remote(
            oh_send.at[q, 0], oh_recv.at[q, 0], oh_ss.at[q, 0], oh_rs.at[q, 0], (outer, j)
        )
        to_outer.start()
        out_o = mm(wt[pl.ds(NINE, NINE), :], vo)
        out_i = mm(wt[pl.ds(inward, NINE), :], vo)
        gather_end(vol, q, 1)
        vi = flat(vol, 1)
        oh_send[q, 1] = fold_taps(mm(wt[pl.ds(inward, NINE), :], vi), h, w)
        to_mate = remote(
            oh_send.at[q, 1], oh_recv.at[q, 1], oh_ss.at[q, 1], oh_rs.at[q, 1], (mate, j)
        )
        to_mate.start()
        send_half(vol, (feat_m, hid_m)[q], q)
        out_o = fold_taps(out_o + mm(wt[pl.ds(away, NINE), :], vi), h, w)
        out_i = fold_taps(out_i + mm(wt[pl.ds(NINE, NINE), :], vi), h, w)
        settle()
        to_outer.wait()
        yield out_o + jnp.where(valid, oh_recv[q, 0], 0.0)
        to_mate.wait()
        yield out_i + oh_recv[q, 1]

    def slope_of(v, sig):
        return sig * (1.0 + v * (1.0 - sig))

    for p in range(2):
        gather_own(feat_hbm.at[core + p - 2 * core * p], feat, 0, p)
    gather_forward(feat, 0)
    for c in locals_:
        c.wait()
    w2[pl.ds(ROWS, PADDED - ROWS), :] = jnp.zeros((PADDED - ROWS, 512), BF)
    for blk in range(PADDED // 128):
        w2t[:, pl.ds(blk * 128, 128)] = w2[pl.ds(blk * 128, 128), :].T
    stack[...] = jnp.zeros_like(stack)
    stack2[pl.ds(0, NINE), :] = jnp.zeros((NINE, PLANE), BF)
    stack2[pl.ds(5 * NINE, NINE + PADDED - ROWS), :] = jnp.zeros((NINE + PADDED - ROWS, PLANE), BF)
    pre = []
    for p, v in enumerate(conv(w1, feat, 0)):
        hid[p, j] = (v * sigmoid(v)).astype(BF).reshape(2, 16, PLANE)
        gather_own(hid.at[p, j], hid, 1, p)
        pre.append(v)
    for p in range(2):
        slope[p] = slope_of(pre[p], sigmoid(pre[p]))
    gather_forward(hid, 1)

    head = head_v[...]
    slopes = []
    for p, v in enumerate(conv(w2, hid, 1)):
        sig = sigmoid(v)
        ly[0, pl.ds(8 * p, 8), :] = mm(head, (v * sig).astype(BF))
        slopes.append(slope_of(v, sig))
    cys = [
        remote(ly.at[0], ly.at[k], c_s.at[0, k], c_r.at[0, k], (s, x * NY + at_y(k)))
        for k in (2, 1, 3)
    ]
    for c in cys:
        c.start()
    nears = send_near()
    for c in cys:
        c.wait()
    lx[0] = (ly[0] + ly[2]) + (ly[1] + ly[3])
    cxs = [
        remote(lx.at[0], lx.at[k], c_s.at[1, k], c_r.at[1, k], (s, at_x(k) * NY + yh))
        for k in (2, 1, 3)
    ]
    for c in cxs:
        c.start()
    for c in cxs:
        c.wait()
    logits = (lx[0] + lx[2]) + (lx[1] + lx[3])
    classes = lax.broadcasted_iota(jnp.int32, (8, PLANE), 0)
    headf = head.astype(F32)
    labels = labels_v[...]
    halos = {}
    own_planes = (3 * core, 1 + core)
    mate_planes = (3 - 3 * core, 2 - core)
    gs = []
    for p in range(2):
        powers = jnp.exp(logits[8 * p : 8 * p + 8])
        likely = powers / jnp.sum(powers, axis=0, keepdims=True)
        row = jnp.where(core == p, labels[0:1], labels[1:2])
        onehot = jnp.where(row == classes, 1.0, 0.0)
        lg = (likely - onehot).astype(BF).astype(F32)
        back = lax.dot_general(headf, lg, (((0,), (0,)), ((), ())), preferred_element_type=F32)
        v = (back * slopes[p]).astype(BF)
        g[p] = v
        if p == 0:
            halos[4] = remote(g.at[0], g.at[4], g_s.at[4], g_r.at[4], (outer, j))
            halos[4].start()
        halos[2 + p] = remote(g.at[p], g.at[2 + p], g_s.at[2 + p], g_r.at[2 + p], (mate, j))
        halos[2 + p].start()
        gs.append(v.astype(F32))
    halos[5] = remote(g.at[0], g.at[5], g_s.at[5], g_r.at[5], (outer_mate, j))
    halos[5].start()
    for p in range(2):
        spread_taps(stack, own_planes[p], gs[p], h, w)

    def term(ref, plane, rows=PADDED, skip=0):
        start = (3 - plane) * NINE + skip
        return ref[pl.ds(start if isinstance(start, int) else pl.multiple_of(start, BLOCK), rows), :]

    def project(p, plane):
        part[p] = mm(w2t[...], term(stack, plane)).astype(BF).reshape(NX, NY, BLOCK, PLANE)
        for k in (2, 1, 3, 0):
            for m in (2, 1, 3):
                c = remote(
                    part.at[p, at_x(m), at_y(k)], rx.at[p, m, k],
                    ex_s.at[p, m, k], ex_r.at[p, m, k], (s, at_x(m) * NY + yh),
                )
                c.start()
                tail.append(c)

    halos[3].wait()
    spread_taps(stack, mate_planes[1], g[3].astype(F32), h, w)
    project(1, own_planes[1])
    halos[4].wait()
    spread_taps(stack, 5 * core - 1, jnp.where(valid, g[4].astype(F32), 0.0), h, w)
    project(0, own_planes[0])

    far = (4, 3, 5, 2, 6)

    def prod(a, b):
        return lax.dot_general(a, b, (((1,), (1,)), ((), ())), preferred_element_type=F32)

    def own_rows(vol, p):
        return vol[p, :, core].reshape(256, PLANE)

    def mate_rows(vol, p):
        return vol[p].reshape(256, PLANE)

    def second_z():
        sent = []
        for k in (4, 3, 5, 2, 6, 1, 7):
            zz = at_z(k)
            sz[k] = wown[0, zz].astype(BF)
            c = remote(
                sz.at[k], rz.at[k], dz_s.at[k], dz_r.at[k], (zz * 4 + yl * 2 + core, j)
            )
            c.start()
            sent.append((k, c))
        return sent

    def second_twin(sent):
        total = wown[0, z]
        for k, c in sent:
            c.wait()
            total = total + rz[k].astype(F32)
        wown[0, z] = total
        st[...] = wown[0, z, 1 - yl].astype(BF)
        c = remote(st, rt, dz_s.at[0], dz_r.at[0], (twin, j))
        c.start()
        return c

    def first_twin():
        sent = {}

        def go(tag, k, src, dst, ss, rs, slab, yy):
            src[k] = wown[1, at_z(k), yy].astype(BF)
            c = remote(src.at[k], dst.at[k], ss.at[k], rs.at[k], (slab, j))
            c.start()
            sent[tag, k] = c

        for k in far:
            go(2, k, s2, r2, a2_s, a2_r, twin, 1 - yl)
        for k in (1, 7):
            go(4, k, s2, r4, a4_s, a4_r, diagonal(k), 1 - yl)
            go(3, k, s3, r3, a3_s, a3_r, at_z(k) * 4 + yl * 2 + core, yl)
        go(2, 0, s2, r2, a2_s, a2_r, twin, 1 - yl)
        return sent

    def first_z(sent):
        for k in far:
            zz = at_z(k)
            sent[2, k].wait()
            s3[k] = (wown[1, zz, yl] + r2[k].astype(F32)).astype(BF)
            c = remote(
                s3.at[k], r3.at[k], a3_s.at[k], a3_r.at[k], (zz * 4 + yl * 2 + core, j)
            )
            c.start()
            sent[3, k] = c

    def first_end(sent):
        total = wown[1, z, yl]
        for ref, tag, k in [(r2, 2, 0), (r4, 4, 1), (r4, 4, 7)] + [
            (r3, 3, k) for k in (1, 7, 4, 3, 5, 2, 6)
        ]:
            sent[tag, k].wait()
            total = total + ref[k].astype(F32)
        out1_ref[...] = total

    mine = [None, None]
    eys = []

    def exchange_y(p):
        for k in (2, 1, 3, 0):
            total = part[p, x, at_y(k)].astype(F32)
            for m in (1, 3, 2):
                slot = rx.at[p, m, k]
                remote(slot, slot, ex_s.at[p, m, k], ex_r.at[p, m, k], (s, j)).wait_recv()
                total = total + rx[p, m, k].astype(F32)
            if k == 0:
                mine[p] = total
            else:
                qs[p, k] = total.astype(BF)
                c = remote(
                    qs.at[p, k], ry.at[p, k], ey_s.at[p, k], ey_r.at[p, k], (s, x * NY + at_y(k))
                )
                c.start()
                eys.append(c)

    halos[2].wait()
    spread_taps(stack, mate_planes[0], g[2].astype(F32), h, w)
    halos[5].wait()
    spread_taps(stack, 4 - 5 * core, jnp.where(far_valid, g[5].astype(F32), 0.0), h, w)
    for c in halves[1]:
        c.wait()
    total = prod(own_rows(hid, 0), term(stack, own_planes[0]))
    total = total + prod(own_rows(hid, 1), term(stack, own_planes[1]))
    total = total + prod(mate_rows(hid_m, 0), term(stack, mate_planes[0]))
    total = total + prod(mate_rows(hid_m, 1), term(stack, mate_planes[1]))
    wown[0] = total.reshape(NZ, 2, 16, PADDED)
    over_z = second_z()
    exchange_y(1)
    exchange_y(0)
    settle()
    swaps = []
    for p in (1, 0):
        for c in eys[3 * (1 - p) : 3 * (1 - p) + 3]:
            c.wait()
        v = mine[p]
        for k in (1, 2, 3):
            v = v + ry[p, k].astype(F32)
        v = (v * slope[p]).astype(BF)
        g2[p] = v
        c = remote(g2.at[p], g2.at[2 + p], g_s.at[p], g_r.at[p], (mate, j))
        c.start()
        swaps.append(c)
        spread_taps(stack2, own_planes[p], v.astype(F32), h, w)
    for c in nears + halves[0]:
        c.wait()
    total = prod(own_rows(feat, 0), term(stack2, own_planes[0]))
    swaps[0].wait()
    spread_taps(stack2, mate_planes[1], g2[3].astype(F32), h, w)
    total = total + prod(own_rows(feat, 1), term(stack2, own_planes[1]))
    swaps[1].wait()
    spread_taps(stack2, mate_planes[0], g2[2].astype(F32), h, w)
    total = total + prod(mate_rows(feat_m, 0), term(stack2, mate_planes[0]))
    total = total + prod(mate_rows(feat_m, 1), term(stack2, mate_planes[1]))
    below = jnp.where(s > 1, mate_rows(near, core), 0.0).astype(BF)
    above = jnp.where(s < n_slab - 2, mate_rows(near, 1 - core), 0.0).astype(BF)
    low = total[:, :384] + prod(below, term(stack2, -1, 384))
    high = total[:, 512:] + prod(above, term(stack2, 4, 384, 512))
    wown[1] = jnp.concatenate([low, total[:, 384:512], high], axis=1).reshape(NZ, 2, 16, PADDED)
    over_twin = first_twin()
    last = second_twin(over_z)
    first_z(over_twin)
    last.wait()
    out2_ref[...] = wown[0, z, yl] + rt[...].astype(F32)
    first_end(over_twin)


def shards(features, first_weight, second_weight, head_weight, labels):
    vmem = pl.BlockSpec(memory_space=pltpu.VMEM)
    hbm = pl.BlockSpec(memory_space=pltpu.HBM)
    dma = pltpu.SemaphoreType.DMA
    out = jax.ShapeDtypeStruct((16, PADDED), F32)
    first, second = pl.pallas_call(
        kernel,
        out_shape=(out, out),
        in_specs=[hbm] * 5,
        out_specs=(vmem, vmem),
        scratch_shapes=[
            pltpu.VMEM((2, 16, 2, 16, PLANE), BF),
            pltpu.VMEM((2, 16, 2, 16, PLANE), BF),
            pltpu.VMEM((2, 16, 16, PLANE), BF),
            pltpu.VMEM((2, 16, 16, PLANE), BF),
            pltpu.VMEM((2, 16, 16, PLANE), BF),
            pltpu.VMEM((ROWS, 512), BF),
            pltpu.VMEM((PADDED, 512), BF),
            pltpu.VMEM((512, PADDED), BF),
            pltpu.VMEM((8, BLOCK), BF),
            pltpu.VMEM((2, PLANE), jnp.int32),
            pltpu.VMEM((2, 2, BLOCK, PLANE), F32),
            pltpu.VMEM((2, 2, BLOCK, PLANE), F32),
            pltpu.VMEM((2, BLOCK, PLANE), F32),
            pltpu.VMEM((4, 16, PLANE), F32),
            pltpu.VMEM((4, 16, PLANE), F32),
            pltpu.VMEM((6, BLOCK, PLANE), BF),
            pltpu.VMEM((4, BLOCK, PLANE), BF),
            pltpu.VMEM((6 * NINE + PADDED - ROWS, PLANE), BF),
            pltpu.VMEM((6 * NINE + PADDED - ROWS, PLANE), BF),
            pltpu.VMEM((2, NX, NY, BLOCK, PLANE), BF),
            pltpu.VMEM((2, NX, NY, BLOCK, PLANE), BF),
            pltpu.VMEM((2, NY, BLOCK, PLANE), BF),
            pltpu.VMEM((2, NY, BLOCK, PLANE), BF),
            pltpu.VMEM((2, NZ, 2, 16, PADDED), F32),
            pltpu.VMEM((NZ, 2, 16, PADDED), BF),
            pltpu.VMEM((NZ, 2, 16, PADDED), BF),
            pltpu.VMEM((16, PADDED), BF),
            pltpu.VMEM((16, PADDED), BF),
            pltpu.VMEM((NZ, 16, PADDED), BF),
            pltpu.VMEM((NZ, 16, PADDED), BF),
            pltpu.VMEM((NZ, 16, PADDED), BF),
            pltpu.VMEM((NZ, 16, PADDED), BF),
            pltpu.VMEM((NZ, 16, PADDED), BF),
            dma((6,)),
            dma((2, 2, 4)), dma((2, 2, 4)), dma((2, 2, 4, 4)), dma((2, 2, 4, 4)),
            dma((2, 2)), dma((2, 2)), dma((2,)), dma((2,)), dma((2, 2)), dma((2, 2)),
            dma((6,)), dma((6,)), dma((2, 4)), dma((2, 4)),
            dma((2, 4, 4)), dma((2, 4, 4)), dma((2, 4)), dma((2, 4)),
            dma((NZ,)), dma((NZ,)), dma((NZ,)), dma((NZ,)), dma((NZ,)), dma((NZ,)), dma((NZ,)), dma((NZ,)),
        ],
        compiler_params=pltpu.CompilerParams(
            collective_id=0, has_side_effects=True, vmem_limit_bytes=60 * 1024 * 1024
        ),
    )(
        features.reshape(2, 2, 16, PLANE),
        first_weight.reshape(ROWS, 512),
        second_weight.reshape(ROWS, 512),
        head_weight,
        labels,
    )
    return tuple(jnp.transpose(v[:, :ROWS]).reshape(27, BLOCK, 16) for v in (first, second))


def solution(mesh):
    placed = (
        P("slab", "filt", None),
        P(None, "filt", None),
        P(None, "filt", None),
        P(None, "filt"),
        P("slab", None),
    )
    return jax.shard_map(
        shards,
        mesh=mesh,
        in_specs=placed,
        out_specs=(P(None, "filt", "slab"), P(None, "filt", "slab")),
        check_vma=False,
    )
```

```python
import functools

import jax
import jax.numpy as jnp
from jax import lax
from jax.experimental import pallas as pl
from jax.experimental.pallas import tpu as pltpu
from jax.sharding import PartitionSpec as P

MESH = pl.DeviceIdType.MESH
WIDTH = 8
HEIGHT = 32
PLANE = 256
NX, NY, NZ = 4, 4, 8
BLOCK = 32
ROWS = 27 * BLOCK
NINE = 9 * BLOCK
PADDED = 896
BF = jnp.bfloat16
F32 = jnp.float32


def sigmoid(v):
    return 1.0 / (1.0 + jnp.exp(-v))


def voxel_masks():
    p = lax.broadcasted_iota(jnp.int32, (BLOCK, PLANE), 1)
    return p // WIDTH, p % WIDTH


def offsets():
    return [(b, e) for b in (-1, 0, 1) for e in (-1, 0, 1)]


def inside(h, w, b, e):
    return (h + b >= 0) & (h + b < HEIGHT) & (w + e >= 0) & (w + e < WIDTH)


def fold_taps(stack, h, w):
    total = stack[4 * BLOCK : 5 * BLOCK]
    for n, (b, e) in enumerate(offsets()):
        if n == 4:
            continue
        moved = pltpu.roll(stack[n * BLOCK : (n + 1) * BLOCK], (-(8 * b + e)) % PLANE, 1)
        total = total + jnp.where(inside(h, w, b, e), moved, 0.0)
    return total


def spread_taps(stack_ref, plane, g, h, w):
    base = pl.multiple_of((4 - plane) * NINE, BLOCK)
    for n, (b, e) in enumerate(offsets()):
        if n == 4:
            moved = g
        else:
            moved = pltpu.roll(g, (8 * b + e) % PLANE, 1)
            moved = jnp.where(inside(h, w, -b, -e), moved, 0.0)
        stack_ref[pl.ds(base + n * BLOCK, BLOCK), :] = moved.astype(BF)


def remote(src, dst, ssem, rsem, dev):
    return pltpu.make_async_remote_copy(
        src_ref=src, dst_ref=dst, send_sem=ssem, recv_sem=rsem, device_id=dev, device_id_type=MESH
    )


def kernel(
    feat_hbm, w1_hbm, w2_hbm, head_hbm, labels_hbm, out1_ref, out2_ref,
    feat, hid, feat_m, hid_m, near, w1, w2, w2t, head_v, labels_v, oh_send, oh_recv, slope, ly, lx, g, g2,
    stack, stack2, part, rx, qs, ry, wown, sz, rz, st, rt, s2, r2, r4, s3, r3,
    local_sem, gy_s, gy_r, gx_s, gx_r, oh_ss, oh_rs, nr_s, nr_r, m_s, m_r, g_s, g_r, c_s, c_r,
    ex_s, ex_r, ey_s, ey_r, dz_s, dz_r, a2_s, a2_r, a3_s, a3_r, a4_s, a4_r,
):
    s = lax.axis_index("slab")
    j = lax.axis_index("filt")
    n_slab = NZ * 4
    x, yh = j // NY, j % NY
    z, yl, core = s // 4, (s // 2) % 2, s % 2

    def at_y(k):
        return (yh + k) % NY

    def at_x(k):
        return (x + k) % NX

    def at_z(k):
        return (z + k) % NZ

    mate = s + 1 - 2 * core
    twin = s + 2 - 4 * yl
    outer = (s + n_slab - 1 + 2 * core) % n_slab
    outer_mate = outer + 1 - 2 * (1 - core)
    valid = (s > 0) & (s < n_slab - 1)
    far_valid = ((core == 1) | (s < n_slab - 2)) & ((core == 0) | (s > 1))

    def diagonal(k):
        return at_z(k) * 4 + (1 - yl) * 2 + core

    locals_ = [
        pltpu.make_async_copy(feat_hbm.at[core], feat.at[0, j], local_sem.at[0]),
        pltpu.make_async_copy(feat_hbm.at[1 - core], feat.at[1, j], local_sem.at[1]),
        pltpu.make_async_copy(w2_hbm, w2.at[pl.ds(0, ROWS)], local_sem.at[2]),
        pltpu.make_async_copy(w1_hbm, w1, local_sem.at[3]),
        pltpu.make_async_copy(head_hbm, head_v, local_sem.at[4]),
        pltpu.make_async_copy(labels_hbm, labels_v, local_sem.at[5]),
    ]

    barrier = pltpu.get_barrier_semaphore()
    peers = [(s, x * NY + at_y(k)) for k in (2, 1, 3)]
    peers += [(s, at_x(k) * NY + yh) for k in (2, 1, 3)]
    peers += [(at_z(k) * 4 + yl * 2 + core, j) for k in (4, 3, 5, 2, 6, 1, 7)]
    peers += [(diagonal(1), j), (diagonal(7), j), (outer, j), (twin, j), (mate, j)]
    for dev in peers:
        pl.semaphore_signal(barrier, inc=1, device_id=dev, device_id_type=MESH)
    for c in locals_:
        c.start()
    pl.semaphore_wait(barrier, len(peers))

    h, w = voxel_masks()
    tail = []

    def gather_own(src, vol, q, p):
        dst = vol.at[p, j]
        sent = []
        for k in (2, 1, 3):
            sent.append(
                remote(src, dst, gy_s.at[q, p, k], gy_r.at[q, p, k], (s, x * NY + at_y(k)))
            )
        for m in (2, 1, 3):
            sent.append(
                remote(src, dst, gx_s.at[q, p, 0, m], gx_r.at[q, p, 0, m], (s, at_x(m) * NY + yh))
            )
        for c in sent:
            c.start()
        tail.extend(sent)

    def gather_forward(vol, q):
        for p, k in ((0, 1), (0, 3), (0, 2), (1, 1), (1, 3), (1, 2)):
            slot = vol.at[p, x * NY + at_y(NY - k)]
            remote(slot, slot, gy_s.at[q, p, k], gy_r.at[q, p, k], (s, j)).wait_recv()
            for m in (2, 1, 3):
                c = remote(
                    slot, slot, gx_s.at[q, p, k, m], gx_r.at[q, p, k, m], (s, at_x(m) * NY + yh)
                )
                c.start()
                tail.append(c)

    def gather_end(vol, q, p):
        for k in (0, 1, 3, 2):
            for m in (1, 3, 2):
                slot = vol.at[p, at_x(NX - m) * NY + at_y(NY - k)]
                remote(slot, slot, gx_s.at[q, p, k, m], gx_r.at[q, p, k, m], (s, j)).wait_recv()

    def settle():
        for c in tail:
            c.wait_send()
        tail.clear()

    def mm(a, b):
        return jnp.dot(a, b, preferred_element_type=F32)

    def flat(vol, p):
        return vol[p].reshape(512, PLANE)

    away = pl.multiple_of((1 - core) * (2 * NINE), BLOCK)
    inward = pl.multiple_of(core * (2 * NINE), BLOCK)

    halves = [[], []]

    def send_near():
        sent = []
        for n, (cls, dev) in enumerate(((1 - core, outer), (core, outer_mate))):
            c = remote(feat.at[0, :, cls], near.at[n], nr_s.at[n], nr_r.at[n], (dev, j))
            c.start()
            sent.append(c)
        return sent

    def send_half(vol, dst, q):
        for p in range(2):
            c = remote(vol.at[p, :, 1 - core], dst.at[p], m_s.at[q, p], m_r.at[q, p], (mate, j))
            c.start()
            halves[q].append(c)

    def conv(wt, vol, q):
        gather_end(vol, q, 0)
        vo = flat(vol, 0)
        oh_send[q, 0] = fold_taps(mm(wt[pl.ds(away, NINE), :], vo), h, w)
        to_outer = remote(
            oh_send.at[q, 0], oh_recv.at[q, 0], oh_ss.at[q, 0], oh_rs.at[q, 0], (outer, j)
        )
        to_outer.start()
        out_o = mm(wt[pl.ds(NINE, NINE), :], vo)
        out_i = mm(wt[pl.ds(inward, NINE), :], vo)
        gather_end(vol, q, 1)
        vi = flat(vol, 1)
        oh_send[q, 1] = fold_taps(mm(wt[pl.ds(inward, NINE), :], vi), h, w)
        to_mate = remote(
            oh_send.at[q, 1], oh_recv.at[q, 1], oh_ss.at[q, 1], oh_rs.at[q, 1], (mate, j)
        )
        to_mate.start()
        send_half(vol, (feat_m, hid_m)[q], q)
        out_o = fold_taps(out_o + mm(wt[pl.ds(away, NINE), :], vi), h, w)
        out_i = fold_taps(out_i + mm(wt[pl.ds(NINE, NINE), :], vi), h, w)
        settle()
        to_outer.wait()
        yield out_o + jnp.where(valid, oh_recv[q, 0], 0.0)
        to_mate.wait()
        yield out_i + oh_recv[q, 1]

    def slope_of(v, sig):
        return sig * (1.0 + v * (1.0 - sig))

    for p in range(2):
        gather_own(feat_hbm.at[core + p - 2 * core * p], feat, 0, p)
    gather_forward(feat, 0)
    for c in locals_:
        c.wait()
    w2[pl.ds(ROWS, PADDED - ROWS), :] = jnp.zeros((PADDED - ROWS, 512), BF)
    for blk in range(PADDED // 128):
        w2t[:, pl.ds(blk * 128, 128)] = w2[pl.ds(blk * 128, 128), :].T
    stack[...] = jnp.zeros_like(stack)
    stack2[pl.ds(0, NINE), :] = jnp.zeros((NINE, PLANE), BF)
    stack2[pl.ds(5 * NINE, NINE + PADDED - ROWS), :] = jnp.zeros((NINE + PADDED - ROWS, PLANE), BF)
    pre = []
    for p, v in enumerate(conv(w1, feat, 0)):
        hid[p, j] = (v * sigmoid(v)).astype(BF).reshape(2, 16, PLANE)
        gather_own(hid.at[p, j], hid, 1, p)
        pre.append(v)
    for p in range(2):
        slope[p] = slope_of(pre[p], sigmoid(pre[p]))
    gather_forward(hid, 1)

    head = head_v[...]
    slopes = []
    for p, v in enumerate(conv(w2, hid, 1)):
        sig = sigmoid(v)
        ly[0, pl.ds(8 * p, 8), :] = mm(head, (v * sig).astype(BF))
        slopes.append(slope_of(v, sig))
    cys = [
        remote(ly.at[0], ly.at[k], c_s.at[0, k], c_r.at[0, k], (s, x * NY + at_y(k)))
        for k in (2, 1, 3)
    ]
    for c in cys:
        c.start()
    nears = send_near()
    for c in cys:
        c.wait()
    lx[0] = (ly[0] + ly[2]) + (ly[1] + ly[3])
    cxs = [
        remote(lx.at[0], lx.at[k], c_s.at[1, k], c_r.at[1, k], (s, at_x(k) * NY + yh))
        for k in (2, 1, 3)
    ]
    for c in cxs:
        c.start()
    for c in cxs:
        c.wait()
    logits = (lx[0] + lx[2]) + (lx[1] + lx[3])
    classes = lax.broadcasted_iota(jnp.int32, (8, PLANE), 0)
    headf = head.astype(F32)
    labels = labels_v[...]
    halos = {}
    own_planes = (3 * core, 1 + core)
    mate_planes = (3 - 3 * core, 2 - core)
    gs = []
    for p in range(2):
        powers = jnp.exp(logits[8 * p : 8 * p + 8])
        likely = powers / jnp.sum(powers, axis=0, keepdims=True)
        row = jnp.where(core == p, labels[0:1], labels[1:2])
        onehot = jnp.where(row == classes, 1.0, 0.0)
        lg = (likely - onehot).astype(BF).astype(F32)
        back = lax.dot_general(headf, lg, (((0,), (0,)), ((), ())), preferred_element_type=F32)
        v = (back * slopes[p]).astype(BF)
        g[p] = v
        if p == 0:
            halos[4] = remote(g.at[0], g.at[4], g_s.at[4], g_r.at[4], (outer, j))
            halos[4].start()
        halos[2 + p] = remote(g.at[p], g.at[2 + p], g_s.at[2 + p], g_r.at[2 + p], (mate, j))
        halos[2 + p].start()
        gs.append(v.astype(F32))
    halos[5] = remote(g.at[0], g.at[5], g_s.at[5], g_r.at[5], (outer_mate, j))
    halos[5].start()
    for p in range(2):
        spread_taps(stack, own_planes[p], gs[p], h, w)

    def term(ref, plane, rows=PADDED, skip=0):
        start = (3 - plane) * NINE + skip
        return ref[pl.ds(start if isinstance(start, int) else pl.multiple_of(start, BLOCK), rows), :]

    def project(p, plane):
        part[p] = mm(w2t[...], term(stack, plane)).astype(BF).reshape(NX, NY, BLOCK, PLANE)
        for k in (2, 1, 3, 0):
            for m in (2, 1, 3):
                c = remote(
                    part.at[p, at_x(m), at_y(k)], rx.at[p, m, k],
                    ex_s.at[p, m, k], ex_r.at[p, m, k], (s, at_x(m) * NY + yh),
                )
                c.start()
                tail.append(c)

    halos[3].wait()
    spread_taps(stack, mate_planes[1], g[3].astype(F32), h, w)
    project(1, own_planes[1])
    halos[4].wait()
    spread_taps(stack, 5 * core - 1, jnp.where(valid, g[4].astype(F32), 0.0), h, w)
    project(0, own_planes[0])

    far = (4, 3, 5, 2, 6)

    def prod(a, b):
        return lax.dot_general(a, b, (((1,), (1,)), ((), ())), preferred_element_type=F32)

    def own_rows(vol, p):
        return vol[p, :, core].reshape(256, PLANE)

    def mate_rows(vol, p):
        return vol[p].reshape(256, PLANE)

    def second_z():
        sent = []
        for k in (4, 3, 5, 2, 6, 1, 7):
            zz = at_z(k)
            sz[k] = wown[0, zz].astype(BF)
            c = remote(
                sz.at[k], rz.at[k], dz_s.at[k], dz_r.at[k], (zz * 4 + yl * 2 + core, j)
            )
            c.start()
            sent.append((k, c))
        return sent

    def second_twin(sent):
        total = wown[0, z]
        for k, c in sent:
            c.wait()
            total = total + rz[k].astype(F32)
        wown[0, z] = total
        st[...] = wown[0, z, 1 - yl].astype(BF)
        c = remote(st, rt, dz_s.at[0], dz_r.at[0], (twin, j))
        c.start()
        return c

    def first_twin():
        sent = {}

        def go(tag, k, src, dst, ss, rs, slab, yy):
            src[k] = wown[1, at_z(k), yy].astype(BF)
            c = remote(src.at[k], dst.at[k], ss.at[k], rs.at[k], (slab, j))
            c.start()
            sent[tag, k] = c

        for k in far:
            go(2, k, s2, r2, a2_s, a2_r, twin, 1 - yl)
        for k in (1, 7):
            go(4, k, s2, r4, a4_s, a4_r, diagonal(k), 1 - yl)
            go(3, k, s3, r3, a3_s, a3_r, at_z(k) * 4 + yl * 2 + core, yl)
        go(2, 0, s2, r2, a2_s, a2_r, twin, 1 - yl)
        return sent

    def first_z(sent):
        for k in far:
            zz = at_z(k)
            sent[2, k].wait()
            s3[k] = (wown[1, zz, yl] + r2[k].astype(F32)).astype(BF)
            c = remote(
                s3.at[k], r3.at[k], a3_s.at[k], a3_r.at[k], (zz * 4 + yl * 2 + core, j)
            )
            c.start()
            sent[3, k] = c

    def first_end(sent):
        total = wown[1, z, yl]
        for ref, tag, k in [(r2, 2, 0), (r4, 4, 1), (r4, 4, 7)] + [
            (r3, 3, k) for k in (1, 7, 4, 3, 5, 2, 6)
        ]:
            sent[tag, k].wait()
            total = total + ref[k].astype(F32)
        out1_ref[...] = total

    mine = [None, None]
    eys = []

    def exchange_y(p):
        for k in (2, 1, 3, 0):
            total = part[p, x, at_y(k)].astype(F32)
            for m in (1, 3, 2):
                slot = rx.at[p, m, k]
                remote(slot, slot, ex_s.at[p, m, k], ex_r.at[p, m, k], (s, j)).wait_recv()
                total = total + rx[p, m, k].astype(F32)
            if k == 0:
                mine[p] = total
            else:
                qs[p, k] = total.astype(BF)
                c = remote(
                    qs.at[p, k], ry.at[p, k], ey_s.at[p, k], ey_r.at[p, k], (s, x * NY + at_y(k))
                )
                c.start()
                eys.append(c)

    halos[2].wait()
    spread_taps(stack, mate_planes[0], g[2].astype(F32), h, w)
    halos[5].wait()
    spread_taps(stack, 4 - 5 * core, jnp.where(far_valid, g[5].astype(F32), 0.0), h, w)
    for c in halves[1]:
        c.wait()
    total = prod(own_rows(hid, 0), term(stack, own_planes[0]))
    total = total + prod(own_rows(hid, 1), term(stack, own_planes[1]))
    total = total + prod(mate_rows(hid_m, 0), term(stack, mate_planes[0]))
    total = total + prod(mate_rows(hid_m, 1), term(stack, mate_planes[1]))
    wown[0] = total.reshape(NZ, 2, 16, PADDED)
    over_z = second_z()
    exchange_y(1)
    exchange_y(0)
    settle()
    swaps = []
    for p in (1, 0):
        for c in eys[3 * (1 - p) : 3 * (1 - p) + 3]:
            c.wait()
        v = mine[p]
        for k in (1, 2, 3):
            v = v + ry[p, k].astype(F32)
        v = (v * slope[p]).astype(BF)
        g2[p] = v
        c = remote(g2.at[p], g2.at[2 + p], g_s.at[p], g_r.at[p], (mate, j))
        c.start()
        swaps.append(c)
        spread_taps(stack2, own_planes[p], v.astype(F32), h, w)
    for c in nears + halves[0]:
        c.wait()
    total = prod(own_rows(feat, 0), term(stack2, own_planes[0]))
    swaps[0].wait()
    spread_taps(stack2, mate_planes[1], g2[3].astype(F32), h, w)
    total = total + prod(own_rows(feat, 1), term(stack2, own_planes[1]))
    swaps[1].wait()
    spread_taps(stack2, mate_planes[0], g2[2].astype(F32), h, w)
    total = total + prod(mate_rows(feat_m, 0), term(stack2, mate_planes[0]))
    total = total + prod(mate_rows(feat_m, 1), term(stack2, mate_planes[1]))
    below = jnp.where(s > 1, mate_rows(near, core), 0.0).astype(BF)
    above = jnp.where(s < n_slab - 2, mate_rows(near, 1 - core), 0.0).astype(BF)
    low = total[:, :384] + prod(below, term(stack2, -1, 384))
    high = total[:, 512:] + prod(above, term(stack2, 4, 384, 512))
    wown[1] = jnp.concatenate([low, total[:, 384:512], high], axis=1).reshape(NZ, 2, 16, PADDED)
    over_twin = first_twin()
    last = second_twin(over_z)
    first_z(over_twin)
    last.wait()
    out2_ref[...] = wown[0, z, yl] + rt[...].astype(F32)
    first_end(over_twin)


def place(first_ref, second_ref, first_out, second_out):
    for src, dst in ((first_ref, first_out), (second_ref, second_out)):
        for t in range(27):
            dst[t] = src[:, t * BLOCK : (t + 1) * BLOCK]


def shards(features, first_weight, second_weight, head_weight, labels):
    vmem = pl.BlockSpec(memory_space=pltpu.VMEM)
    hbm = pl.BlockSpec(memory_space=pltpu.HBM)
    dma = pltpu.SemaphoreType.DMA
    out = jax.ShapeDtypeStruct((16, PADDED), F32)
    first, second = pl.pallas_call(
        kernel,
        out_shape=(out, out),
        in_specs=[hbm] * 5,
        out_specs=(vmem, vmem),
        scratch_shapes=[
            pltpu.VMEM((2, 16, 2, 16, PLANE), BF),
            pltpu.VMEM((2, 16, 2, 16, PLANE), BF),
            pltpu.VMEM((2, 16, 16, PLANE), BF),
            pltpu.VMEM((2, 16, 16, PLANE), BF),
            pltpu.VMEM((2, 16, 16, PLANE), BF),
            pltpu.VMEM((ROWS, 512), BF),
            pltpu.VMEM((PADDED, 512), BF),
            pltpu.VMEM((512, PADDED), BF),
            pltpu.VMEM((8, BLOCK), BF),
            pltpu.VMEM((2, PLANE), jnp.int32),
            pltpu.VMEM((2, 2, BLOCK, PLANE), F32),
            pltpu.VMEM((2, 2, BLOCK, PLANE), F32),
            pltpu.VMEM((2, BLOCK, PLANE), F32),
            pltpu.VMEM((4, 16, PLANE), F32),
            pltpu.VMEM((4, 16, PLANE), F32),
            pltpu.VMEM((6, BLOCK, PLANE), BF),
            pltpu.VMEM((4, BLOCK, PLANE), BF),
            pltpu.VMEM((6 * NINE + PADDED - ROWS, PLANE), BF),
            pltpu.VMEM((6 * NINE + PADDED - ROWS, PLANE), BF),
            pltpu.VMEM((2, NX, NY, BLOCK, PLANE), BF),
            pltpu.VMEM((2, NX, NY, BLOCK, PLANE), BF),
            pltpu.VMEM((2, NY, BLOCK, PLANE), BF),
            pltpu.VMEM((2, NY, BLOCK, PLANE), BF),
            pltpu.VMEM((2, NZ, 2, 16, PADDED), F32),
            pltpu.VMEM((NZ, 2, 16, PADDED), BF),
            pltpu.VMEM((NZ, 2, 16, PADDED), BF),
            pltpu.VMEM((16, PADDED), BF),
            pltpu.VMEM((16, PADDED), BF),
            pltpu.VMEM((NZ, 16, PADDED), BF),
            pltpu.VMEM((NZ, 16, PADDED), BF),
            pltpu.VMEM((NZ, 16, PADDED), BF),
            pltpu.VMEM((NZ, 16, PADDED), BF),
            pltpu.VMEM((NZ, 16, PADDED), BF),
            dma((6,)),
            dma((2, 2, 4)), dma((2, 2, 4)), dma((2, 2, 4, 4)), dma((2, 2, 4, 4)),
            dma((2, 2)), dma((2, 2)), dma((2,)), dma((2,)), dma((2, 2)), dma((2, 2)),
            dma((6,)), dma((6,)), dma((2, 4)), dma((2, 4)),
            dma((2, 4, 4)), dma((2, 4, 4)), dma((2, 4)), dma((2, 4)),
            dma((NZ,)), dma((NZ,)), dma((NZ,)), dma((NZ,)), dma((NZ,)), dma((NZ,)), dma((NZ,)), dma((NZ,)),
        ],
        compiler_params=pltpu.CompilerParams(
            collective_id=0, has_side_effects=True, vmem_limit_bytes=60 * 1024 * 1024
        ),
    )(
        features.reshape(2, 2, 16, PLANE),
        first_weight.reshape(ROWS, 512),
        second_weight.reshape(ROWS, 512),
        head_weight,
        labels,
    )
    placed = jax.ShapeDtypeStruct((27, 16, BLOCK), F32)
    outs = pl.pallas_call(
        place,
        out_shape=(placed, placed),
        in_specs=[vmem, vmem],
        out_specs=(vmem, vmem),
    )(first, second)
    return tuple(jnp.swapaxes(v, 1, 2) for v in outs)


def solution(mesh):
    placed = (
        P("slab", "filt", None),
        P(None, "filt", None),
        P(None, "filt", None),
        P(None, "filt"),
        P("slab", None),
    )
    return jax.shard_map(
        shards,
        mesh=mesh,
        in_specs=placed,
        out_specs=(P(None, "filt", "slab"), P(None, "filt", "slab")),
        check_vma=False,
    )
```

```python
import functools

import jax
import jax.numpy as jnp
from jax import lax
from jax.experimental import pallas as pl
from jax.experimental.pallas import tpu as pltpu
from jax.sharding import PartitionSpec as P

MESH = pl.DeviceIdType.MESH
WIDTH = 8
HEIGHT = 32
PLANE = 256
NX, NY, NZ = 4, 4, 8
BLOCK = 32
ROWS = 27 * BLOCK
NINE = 9 * BLOCK
PADDED = 896
BF = jnp.bfloat16
F32 = jnp.float32


def sigmoid(v):
    return 1.0 / (1.0 + jnp.exp(-v))


def voxel_masks():
    p = lax.broadcasted_iota(jnp.int32, (BLOCK, PLANE), 1)
    return p // WIDTH, p % WIDTH


def offsets():
    return [(b, e) for b in (-1, 0, 1) for e in (-1, 0, 1)]


def inside(h, w, b, e):
    return (h + b >= 0) & (h + b < HEIGHT) & (w + e >= 0) & (w + e < WIDTH)


def fold_taps(stack, h, w):
    total = stack[4 * BLOCK : 5 * BLOCK]
    for n, (b, e) in enumerate(offsets()):
        if n == 4:
            continue
        moved = pltpu.roll(stack[n * BLOCK : (n + 1) * BLOCK], (-(8 * b + e)) % PLANE, 1)
        total = total + jnp.where(inside(h, w, b, e), moved, 0.0)
    return total


def spread_taps(stack_ref, plane, g, h, w):
    base = pl.multiple_of((4 - plane) * NINE, BLOCK)
    for n, (b, e) in enumerate(offsets()):
        if n == 4:
            moved = g
        else:
            moved = pltpu.roll(g, (8 * b + e) % PLANE, 1)
            moved = jnp.where(inside(h, w, -b, -e), moved, 0.0)
        stack_ref[pl.ds(base + n * BLOCK, BLOCK), :] = moved.astype(BF)


def remote(src, dst, ssem, rsem, dev):
    return pltpu.make_async_remote_copy(
        src_ref=src, dst_ref=dst, send_sem=ssem, recv_sem=rsem, device_id=dev, device_id_type=MESH
    )


def kernel(
    feat_hbm, w1_hbm, w2_hbm, head_hbm, labels_hbm, out1_ref, out2_ref,
    feat, hid, feat_m, hid_m, near, w1, w2, w2t, head_v, labels_v, oh_send, oh_recv, slope, ly, lx, g, g2,
    stack, stack2, part, rx, qs, ry, wown, sz, rz, st, rt, s2, r2, r4, s3, r3,
    local_sem, gy_s, gy_r, gx_s, gx_r, oh_ss, oh_rs, nr_s, nr_r, m_s, m_r, g_s, g_r, c_s, c_r,
    ex_s, ex_r, ey_s, ey_r, dz_s, dz_r, a2_s, a2_r, a3_s, a3_r, a4_s, a4_r,
):
    s = lax.axis_index("slab")
    j = lax.axis_index("filt")
    n_slab = NZ * 4
    x, yh = j // NY, j % NY
    z, yl, core = s // 4, (s // 2) % 2, s % 2

    def at_y(k):
        return (yh + k) % NY

    def at_x(k):
        return (x + k) % NX

    def at_z(k):
        return (z + k) % NZ

    mate = s + 1 - 2 * core
    twin = s + 2 - 4 * yl
    outer = (s + n_slab - 1 + 2 * core) % n_slab
    outer_mate = outer + 1 - 2 * (1 - core)
    valid = (s > 0) & (s < n_slab - 1)
    far_valid = ((core == 1) | (s < n_slab - 2)) & ((core == 0) | (s > 1))

    def diagonal(k):
        return at_z(k) * 4 + (1 - yl) * 2 + core

    locals_ = [
        pltpu.make_async_copy(feat_hbm.at[core], feat.at[0, j], local_sem.at[0]),
        pltpu.make_async_copy(feat_hbm.at[1 - core], feat.at[1, j], local_sem.at[1]),
        pltpu.make_async_copy(w2_hbm, w2.at[pl.ds(0, ROWS)], local_sem.at[2]),
        pltpu.make_async_copy(w1_hbm, w1, local_sem.at[3]),
        pltpu.make_async_copy(head_hbm, head_v, local_sem.at[4]),
        pltpu.make_async_copy(labels_hbm, labels_v, local_sem.at[5]),
    ]

    barrier = pltpu.get_barrier_semaphore()
    peers = [(s, x * NY + at_y(k)) for k in (2, 1, 3)]
    peers += [(s, at_x(k) * NY + yh) for k in (2, 1, 3)]
    peers += [(at_z(k) * 4 + yl * 2 + core, j) for k in (4, 3, 5, 2, 6, 1, 7)]
    peers += [(diagonal(2), j), (diagonal(6), j), (diagonal(1), j), (diagonal(7), j), (outer, j), (twin, j), (mate, j)]
    for dev in peers:
        pl.semaphore_signal(barrier, inc=1, device_id=dev, device_id_type=MESH)
    for c in locals_:
        c.start()
    pl.semaphore_wait(barrier, len(peers))

    h, w = voxel_masks()
    tail = []

    def gather_own(src, vol, q, p):
        dst = vol.at[p, j]
        sent = []
        for k in (2, 1, 3):
            sent.append(
                remote(src, dst, gy_s.at[q, p, k], gy_r.at[q, p, k], (s, x * NY + at_y(k)))
            )
        for m in (2, 1, 3):
            sent.append(
                remote(src, dst, gx_s.at[q, p, 0, m], gx_r.at[q, p, 0, m], (s, at_x(m) * NY + yh))
            )
        for c in sent:
            c.start()
        tail.extend(sent)

    def gather_forward(vol, q):
        for p, k in ((0, 1), (0, 3), (0, 2), (1, 1), (1, 3), (1, 2)):
            slot = vol.at[p, x * NY + at_y(NY - k)]
            remote(slot, slot, gy_s.at[q, p, k], gy_r.at[q, p, k], (s, j)).wait_recv()
            for m in (2, 1, 3):
                c = remote(
                    slot, slot, gx_s.at[q, p, k, m], gx_r.at[q, p, k, m], (s, at_x(m) * NY + yh)
                )
                c.start()
                tail.append(c)

    def gather_end(vol, q, p):
        for k in (0, 1, 3, 2):
            for m in (1, 3, 2):
                slot = vol.at[p, at_x(NX - m) * NY + at_y(NY - k)]
                remote(slot, slot, gx_s.at[q, p, k, m], gx_r.at[q, p, k, m], (s, j)).wait_recv()

    def settle():
        for c in tail:
            c.wait_send()
        tail.clear()

    def mm(a, b):
        return jnp.dot(a, b, preferred_element_type=F32)

    def flat(vol, p):
        return vol[p].reshape(512, PLANE)

    away = pl.multiple_of((1 - core) * (2 * NINE), BLOCK)
    inward = pl.multiple_of(core * (2 * NINE), BLOCK)

    halves = [[], []]

    def send_near():
        sent = []
        for n, (cls, dev) in enumerate(((1 - core, outer), (core, outer_mate))):
            c = remote(feat.at[0, :, cls], near.at[n], nr_s.at[n], nr_r.at[n], (dev, j))
            c.start()
            sent.append(c)
        return sent

    def send_half(vol, dst, q):
        for p in range(2):
            c = remote(vol.at[p, :, 1 - core], dst.at[p], m_s.at[q, p], m_r.at[q, p], (mate, j))
            c.start()
            halves[q].append(c)

    def conv(wt, vol, q):
        gather_end(vol, q, 0)
        vo = flat(vol, 0)
        oh_send[q, 0] = fold_taps(mm(wt[pl.ds(away, NINE), :], vo), h, w)
        to_outer = remote(
            oh_send.at[q, 0], oh_recv.at[q, 0], oh_ss.at[q, 0], oh_rs.at[q, 0], (outer, j)
        )
        to_outer.start()
        out_o = mm(wt[pl.ds(NINE, NINE), :], vo)
        out_i = mm(wt[pl.ds(inward, NINE), :], vo)
        gather_end(vol, q, 1)
        vi = flat(vol, 1)
        oh_send[q, 1] = fold_taps(mm(wt[pl.ds(inward, NINE), :], vi), h, w)
        to_mate = remote(
            oh_send.at[q, 1], oh_recv.at[q, 1], oh_ss.at[q, 1], oh_rs.at[q, 1], (mate, j)
        )
        to_mate.start()
        send_half(vol, (feat_m, hid_m)[q], q)
        out_o = fold_taps(out_o + mm(wt[pl.ds(away, NINE), :], vi), h, w)
        out_i = fold_taps(out_i + mm(wt[pl.ds(NINE, NINE), :], vi), h, w)
        settle()
        to_outer.wait()
        yield out_o + jnp.where(valid, oh_recv[q, 0], 0.0)
        to_mate.wait()
        yield out_i + oh_recv[q, 1]

    def slope_of(v, sig):
        return sig * (1.0 + v * (1.0 - sig))

    for p in range(2):
        gather_own(feat_hbm.at[core + p - 2 * core * p], feat, 0, p)
    gather_forward(feat, 0)
    for c in locals_:
        c.wait()
    w2[pl.ds(ROWS, PADDED - ROWS), :] = jnp.zeros((PADDED - ROWS, 512), BF)
    for blk in range(PADDED // 128):
        w2t[:, pl.ds(blk * 128, 128)] = w2[pl.ds(blk * 128, 128), :].T
    stack[...] = jnp.zeros_like(stack)
    stack2[pl.ds(0, NINE), :] = jnp.zeros((NINE, PLANE), BF)
    stack2[pl.ds(5 * NINE, NINE + PADDED - ROWS), :] = jnp.zeros((NINE + PADDED - ROWS, PLANE), BF)
    pre = []
    for p, v in enumerate(conv(w1, feat, 0)):
        hid[p, j] = (v * sigmoid(v)).astype(BF).reshape(2, 16, PLANE)
        gather_own(hid.at[p, j], hid, 1, p)
        pre.append(v)
    for p in range(2):
        slope[p] = slope_of(pre[p], sigmoid(pre[p]))
    gather_forward(hid, 1)

    head = head_v[...]
    slopes = []
    for p, v in enumerate(conv(w2, hid, 1)):
        sig = sigmoid(v)
        ly[0, pl.ds(8 * p, 8), :] = mm(head, (v * sig).astype(BF))
        slopes.append(slope_of(v, sig))
    cys = [
        remote(ly.at[0], ly.at[k], c_s.at[0, k], c_r.at[0, k], (s, x * NY + at_y(k)))
        for k in (2, 1, 3)
    ]
    for c in cys:
        c.start()
    nears = send_near()
    for c in cys:
        c.wait()
    lx[0] = (ly[0] + ly[2]) + (ly[1] + ly[3])
    cxs = [
        remote(lx.at[0], lx.at[k], c_s.at[1, k], c_r.at[1, k], (s, at_x(k) * NY + yh))
        for k in (2, 1, 3)
    ]
    for c in cxs:
        c.start()
    for c in cxs:
        c.wait()
    logits = (lx[0] + lx[2]) + (lx[1] + lx[3])
    classes = lax.broadcasted_iota(jnp.int32, (8, PLANE), 0)
    headf = head.astype(F32)
    labels = labels_v[...]
    halos = {}
    own_planes = (3 * core, 1 + core)
    mate_planes = (3 - 3 * core, 2 - core)
    gs = []
    for p in range(2):
        powers = jnp.exp(logits[8 * p : 8 * p + 8])
        likely = powers / jnp.sum(powers, axis=0, keepdims=True)
        row = jnp.where(core == p, labels[0:1], labels[1:2])
        onehot = jnp.where(row == classes, 1.0, 0.0)
        lg = (likely - onehot).astype(BF).astype(F32)
        back = lax.dot_general(headf, lg, (((0,), (0,)), ((), ())), preferred_element_type=F32)
        v = (back * slopes[p]).astype(BF)
        g[p] = v
        if p == 0:
            halos[4] = remote(g.at[0], g.at[4], g_s.at[4], g_r.at[4], (outer, j))
            halos[4].start()
        halos[2 + p] = remote(g.at[p], g.at[2 + p], g_s.at[2 + p], g_r.at[2 + p], (mate, j))
        halos[2 + p].start()
        gs.append(v.astype(F32))
    halos[5] = remote(g.at[0], g.at[5], g_s.at[5], g_r.at[5], (outer_mate, j))
    halos[5].start()
    for p in range(2):
        spread_taps(stack, own_planes[p], gs[p], h, w)

    def term(ref, plane, rows=PADDED, skip=0):
        start = (3 - plane) * NINE + skip
        return ref[pl.ds(start if isinstance(start, int) else pl.multiple_of(start, BLOCK), rows), :]

    def project(p, plane):
        part[p] = mm(w2t[...], term(stack, plane)).astype(BF).reshape(NX, NY, BLOCK, PLANE)
        for k in (2, 1, 3, 0):
            for m in (2, 1, 3):
                c = remote(
                    part.at[p, at_x(m), at_y(k)], rx.at[p, m, k],
                    ex_s.at[p, m, k], ex_r.at[p, m, k], (s, at_x(m) * NY + yh),
                )
                c.start()
                tail.append(c)

    halos[3].wait()
    spread_taps(stack, mate_planes[1], g[3].astype(F32), h, w)
    project(1, own_planes[1])
    halos[4].wait()
    spread_taps(stack, 5 * core - 1, jnp.where(valid, g[4].astype(F32), 0.0), h, w)
    project(0, own_planes[0])

    far = (4, 3, 5, 2)
    close = (6, 1, 7)

    def prod(a, b):
        return lax.dot_general(a, b, (((1,), (1,)), ((), ())), preferred_element_type=F32)

    def own_rows(vol, p):
        return vol[p, :, core].reshape(256, PLANE)

    def mate_rows(vol, p):
        return vol[p].reshape(256, PLANE)

    def second_z():
        sent = []
        for k in (4, 3, 5, 2, 6, 1, 7):
            zz = at_z(k)
            sz[k] = wown[0, zz].astype(BF)
            c = remote(
                sz.at[k], rz.at[k], dz_s.at[k], dz_r.at[k], (zz * 4 + yl * 2 + core, j)
            )
            c.start()
            sent.append((k, c))
        return sent

    def second_twin(sent):
        total = wown[0, z]
        for k, c in sent:
            c.wait()
            total = total + rz[k].astype(F32)
        wown[0, z] = total
        st[...] = wown[0, z, 1 - yl].astype(BF)
        c = remote(st, rt, dz_s.at[0], dz_r.at[0], (twin, j))
        c.start()
        return c

    def first_twin(sent, ks):
        def go(tag, k, src, dst, ss, rs, slab, yy):
            src[k] = wown[1, at_z(k), yy].astype(BF)
            c = remote(src.at[k], dst.at[k], ss.at[k], rs.at[k], (slab, j))
            c.start()
            sent[tag, k] = c

        for k in ks:
            if k in close:
                go(4, k, s2, r4, a4_s, a4_r, diagonal(k), 1 - yl)
                go(3, k, s3, r3, a3_s, a3_r, at_z(k) * 4 + yl * 2 + core, yl)
            else:
                go(2, k, s2, r2, a2_s, a2_r, twin, 1 - yl)

    def first_z(sent):
        for k in far:
            zz = at_z(k)
            sent[2, k].wait()
            s3[k] = (wown[1, zz, yl] + r2[k].astype(F32)).astype(BF)
            c = remote(
                s3.at[k], r3.at[k], a3_s.at[k], a3_r.at[k], (zz * 4 + yl * 2 + core, j)
            )
            c.start()
            sent[3, k] = c

    def first_end(sent):
        total = wown[1, z, yl]
        for ref, tag, k in [(r2, 2, 0)] + [(r4, 4, k) for k in close] + [
            (r3, 3, k) for k in close + far
        ]:
            sent[tag, k].wait()
            total = total + ref[k].astype(F32)
        out1_ref[...] = total

    mine = [None, None]
    eys = []

    def exchange_y(p):
        for k in (2, 1, 3, 0):
            total = part[p, x, at_y(k)].astype(F32)
            for m in (1, 3, 2):
                slot = rx.at[p, m, k]
                remote(slot, slot, ex_s.at[p, m, k], ex_r.at[p, m, k], (s, j)).wait_recv()
                total = total + rx[p, m, k].astype(F32)
            if k == 0:
                mine[p] = total
            else:
                qs[p, k] = total.astype(BF)
                c = remote(
                    qs.at[p, k], ry.at[p, k], ey_s.at[p, k], ey_r.at[p, k], (s, x * NY + at_y(k))
                )
                c.start()
                eys.append(c)

    halos[2].wait()
    spread_taps(stack, mate_planes[0], g[2].astype(F32), h, w)
    halos[5].wait()
    spread_taps(stack, 4 - 5 * core, jnp.where(far_valid, g[5].astype(F32), 0.0), h, w)
    for c in halves[1]:
        c.wait()
    total = prod(own_rows(hid, 0), term(stack, own_planes[0]))
    total = total + prod(own_rows(hid, 1), term(stack, own_planes[1]))
    total = total + prod(mate_rows(hid_m, 0), term(stack, mate_planes[0]))
    total = total + prod(mate_rows(hid_m, 1), term(stack, mate_planes[1]))
    wown[0] = total.reshape(NZ, 2, 16, PADDED)
    over_z = second_z()
    exchange_y(1)
    exchange_y(0)
    settle()
    swaps = []
    for p in (1, 0):
        for c in eys[3 * (1 - p) : 3 * (1 - p) + 3]:
            c.wait()
        v = mine[p]
        for k in (1, 2, 3):
            v = v + ry[p, k].astype(F32)
        v = (v * slope[p]).astype(BF)
        g2[p] = v
        c = remote(g2.at[p], g2.at[2 + p], g_s.at[p], g_r.at[p], (mate, j))
        c.start()
        swaps.append(c)
        spread_taps(stack2, own_planes[p], v.astype(F32), h, w)
    for c in nears + halves[0]:
        c.wait()
    def rows_of(vol, p, ks, *cls):
        picked = [vol[(p, pl.ds(2 * at_z(k), 2)) + cls] for k in ks]
        return jnp.concatenate(picked, axis=0).reshape(32 * len(ks), PLANE)

    over_twin = {}
    for n, ks in enumerate((far, close + (0,))):
        total = prod(rows_of(feat, 0, ks, core), term(stack2, own_planes[0]))
        if n == 0:
            swaps[0].wait()
            spread_taps(stack2, mate_planes[1], g2[3].astype(F32), h, w)
        total = total + prod(rows_of(feat, 1, ks, core), term(stack2, own_planes[1]))
        if n == 0:
            swaps[1].wait()
            spread_taps(stack2, mate_planes[0], g2[2].astype(F32), h, w)
        total = total + prod(rows_of(feat_m, 0, ks), term(stack2, mate_planes[0]))
        total = total + prod(rows_of(feat_m, 1, ks), term(stack2, mate_planes[1]))
        below = jnp.where(s > 1, rows_of(near, core, ks), 0.0).astype(BF)
        above = jnp.where(s < n_slab - 2, rows_of(near, 1 - core, ks), 0.0).astype(BF)
        low = total[:, :384] + prod(below, term(stack2, -1, 384))
        high = total[:, 512:] + prod(above, term(stack2, 4, 384, 512))
        total = jnp.concatenate([low, total[:, 384:512], high], axis=1)
        for i, k in enumerate(ks):
            wown[1, at_z(k)] = total[32 * i : 32 * (i + 1)].reshape(2, 16, PADDED)
        first_twin(over_twin, ks)
    last = second_twin(over_z)
    first_z(over_twin)
    last.wait()
    out2_ref[...] = wown[0, z, yl] + rt[...].astype(F32)
    first_end(over_twin)


def place(first_ref, second_ref, first_out, second_out):
    for src, dst in ((first_ref, first_out), (second_ref, second_out)):
        for t in range(27):
            dst[t] = src[:, t * BLOCK : (t + 1) * BLOCK]


def shards(features, first_weight, second_weight, head_weight, labels):
    vmem = pl.BlockSpec(memory_space=pltpu.VMEM)
    hbm = pl.BlockSpec(memory_space=pltpu.HBM)
    dma = pltpu.SemaphoreType.DMA
    out = jax.ShapeDtypeStruct((16, PADDED), F32)
    first, second = pl.pallas_call(
        kernel,
        out_shape=(out, out),
        in_specs=[hbm] * 5,
        out_specs=(vmem, vmem),
        scratch_shapes=[
            pltpu.VMEM((2, 16, 2, 16, PLANE), BF),
            pltpu.VMEM((2, 16, 2, 16, PLANE), BF),
            pltpu.VMEM((2, 16, 16, PLANE), BF),
            pltpu.VMEM((2, 16, 16, PLANE), BF),
            pltpu.VMEM((2, 16, 16, PLANE), BF),
            pltpu.VMEM((ROWS, 512), BF),
            pltpu.VMEM((PADDED, 512), BF),
            pltpu.VMEM((512, PADDED), BF),
            pltpu.VMEM((8, BLOCK), BF),
            pltpu.VMEM((2, PLANE), jnp.int32),
            pltpu.VMEM((2, 2, BLOCK, PLANE), F32),
            pltpu.VMEM((2, 2, BLOCK, PLANE), F32),
            pltpu.VMEM((2, BLOCK, PLANE), F32),
            pltpu.VMEM((4, 16, PLANE), F32),
            pltpu.VMEM((4, 16, PLANE), F32),
            pltpu.VMEM((6, BLOCK, PLANE), BF),
            pltpu.VMEM((4, BLOCK, PLANE), BF),
            pltpu.VMEM((6 * NINE + PADDED - ROWS, PLANE), BF),
            pltpu.VMEM((6 * NINE + PADDED - ROWS, PLANE), BF),
            pltpu.VMEM((2, NX, NY, BLOCK, PLANE), BF),
            pltpu.VMEM((2, NX, NY, BLOCK, PLANE), BF),
            pltpu.VMEM((2, NY, BLOCK, PLANE), BF),
            pltpu.VMEM((2, NY, BLOCK, PLANE), BF),
            pltpu.VMEM((2, NZ, 2, 16, PADDED), F32),
            pltpu.VMEM((NZ, 2, 16, PADDED), BF),
            pltpu.VMEM((NZ, 2, 16, PADDED), BF),
            pltpu.VMEM((16, PADDED), BF),
            pltpu.VMEM((16, PADDED), BF),
            pltpu.VMEM((NZ, 16, PADDED), BF),
            pltpu.VMEM((NZ, 16, PADDED), BF),
            pltpu.VMEM((NZ, 16, PADDED), BF),
            pltpu.VMEM((NZ, 16, PADDED), BF),
            pltpu.VMEM((NZ, 16, PADDED), BF),
            dma((6,)),
            dma((2, 2, 4)), dma((2, 2, 4)), dma((2, 2, 4, 4)), dma((2, 2, 4, 4)),
            dma((2, 2)), dma((2, 2)), dma((2,)), dma((2,)), dma((2, 2)), dma((2, 2)),
            dma((6,)), dma((6,)), dma((2, 4)), dma((2, 4)),
            dma((2, 4, 4)), dma((2, 4, 4)), dma((2, 4)), dma((2, 4)),
            dma((NZ,)), dma((NZ,)), dma((NZ,)), dma((NZ,)), dma((NZ,)), dma((NZ,)), dma((NZ,)), dma((NZ,)),
        ],
        compiler_params=pltpu.CompilerParams(
            collective_id=0, has_side_effects=True, vmem_limit_bytes=60 * 1024 * 1024
        ),
    )(
        features.reshape(2, 2, 16, PLANE),
        first_weight.reshape(ROWS, 512),
        second_weight.reshape(ROWS, 512),
        head_weight,
        labels,
    )
    placed = jax.ShapeDtypeStruct((27, 16, BLOCK), F32)
    outs = pl.pallas_call(
        place,
        out_shape=(placed, placed),
        in_specs=[vmem, vmem],
        out_specs=(vmem, vmem),
    )(first, second)
    return tuple(jnp.swapaxes(v, 1, 2) for v in outs)


def solution(mesh):
    placed = (
        P("slab", "filt", None),
        P(None, "filt", None),
        P(None, "filt", None),
        P(None, "filt"),
        P("slab", None),
    )
    return jax.shard_map(
        shards,
        mesh=mesh,
        in_specs=placed,
        out_specs=(P(None, "filt", "slab"), P(None, "filt", "slab")),
        check_vma=False,
    )
```
